256 devices in a mesh: obs: 32 (over z, x_hi, core), ind: 8 (over y, x_lo).
Axes of the slice: x: 4 (x_hi: 2, x_lo: 2; x = x_hi * 2 + x_lo), y: 4, z: 8, core: 2. Of those that a mesh axis runs over, the one named last changes fastest.
Arguments:
- obs_coords: float32 [2, 131072], P(None, 'obs'), may hold values from 0 to 1
- obs_codes: int32 [131072], P('obs'), may hold values from 0 to 47
- route_plan: int32 [32, 32], replicated, may hold values from 0 to 1, as said below
- inducing_coords: float32 [2, 8192], P(None, 'ind'), may hold values from 0 to 1
- inducing_bands: int32 [8192], P('ind'), may hold values from 0 to 5
- band_mix: float32 [6, 6], replicated, may hold values from -2.4 to 2.4
- lengthscales: float32 [2], replicated, may hold values from 0.04 to 0.1
- class_scales: float32 [8], replicated, may hold values from 0.5 to 2
- prior_factor: bfloat16 [8192, 1024], P(('ind', 'obs')), may hold values from -0.046875 to 0.046875
- variational_chol: bfloat16 [8192, 1024], P(('ind', 'obs')), may hold values from -1 to 1, as said below
- variational_mean: bfloat16 [8, 8192], P(None, 'ind'), may hold values from -6 to 6
Outputs:
- class_probs: float32 [8, 65536], P(None, 'obs')
- grad_chol: float32 [8192, 1024], P(('ind', 'obs'))
- grad_mean: float32 [8, 8192], P(None, 'ind')
The draws below stay inside these ranges and needn't reach their ends.
Inputs may be any that keep to these rules, and one draw needn't show every extreme that they name: `route_plan`: entry [s, d] is the number of 128-row blocks that reader s hands to device d; every column sums to 16; a reader's blocks go out in order of destination from the front of its buffer. `variational_chol`: each block's rows are lower triangular within the block, with diagonal entries of 0.3 to 1.
All inputs are finite; a program needn't handle non-finite values.
Results may differ from the reference program's by a relative error of at most 0.014.
Values may be sent and summed in bfloat16 or wider, within the bound.
A program may use at most 64 MiB of HBM per device.

```python
import math
import jax
import jax.numpy as jnp
from jax import lax

MB = 1024
C = 8
NB = 6
ROWS_DEV = 2048
M = 8192
READ_BUF = 131072
N_OBS = 32
N_IND = 8


def draw_route_plan(key, part):
    quota = ROWS_DEV // 128
    first, second = jax.random.split(jax.random.fold_in(key, 11))
    bias = jax.random.randint(first, (N_OBS, 1), 0, 4)
    noise = jax.random.randint(second, (N_OBS, N_OBS), 0, 1 << 20)
    sources = jnp.arange(N_OBS, dtype=jnp.int32)
    score = (bias * (1 << 20) + noise) * 64 + sources[:, None]
    chosen = lax.top_k(score.T, quota)[1]
    hits = jnp.sum((chosen[:, :, None] == sources[None, None, :]).astype(jnp.int32), axis=1)
    return hits.T.astype(jnp.int32)


def draw_variational_chol(key, part):
    first, second = jax.random.split(jax.random.fold_in(key, 23))
    row_ids = jnp.arange(M, dtype=jnp.int32)[:, None] % MB
    column_ids = jnp.arange(MB, dtype=jnp.int32)[None, :]
    diagonal = jax.random.uniform(first, (M, MB), jnp.float32, 0.3, 1.0)
    spread = jnp.clip(jax.random.normal(second, (M, MB), jnp.float32) * (0.6 / MB ** 0.5), -1.0, 1.0)
    value = jnp.where(column_ids == row_ids, diagonal, jnp.where(column_ids < row_ids, spread, 0.0))
    return value.astype(jnp.bfloat16)


def place_ends(values, stream_key, smallest, top_value):
    longest = values.shape.index(max(values.shape))
    spots = []
    for shift in (0, 1):
        where = [jax.random.randint(jax.random.fold_in(stream_key, axis), (), 0, length) for axis, length in enumerate(values.shape)]
        where[longest] = (where[longest] + shift) % values.shape[longest]
        spots.append(tuple(where))
    return values.at[spots[0]].set(smallest).at[spots[1]].set(top_value)


def steps_of(rng, shape, cuts, low, top_value):
    def one(axis_at, blocks):
        steps = jax.random.uniform(jax.random.fold_in(jax.random.fold_in(rng, 6), axis_at), (blocks,), jnp.float32, low / len(cuts), top_value / len(cuts))
        return jnp.repeat(jnp.exp(steps), shape[axis_at] // blocks).reshape((-1,) + (1,) * (len(shape) - axis_at - 1))

    factor_of = one(*cuts[0])
    for cut in cuts[1:]:
        factor_of = factor_of * one(*cut)
    return factor_of


def normal_values(stream_key, extent, width, reach, cuts=(), held_as=jnp.bfloat16):
    drawn = jax.random.normal(stream_key, extent, jnp.float32) * width
    if len(cuts) > 0:
        drawn = steps_of(stream_key, extent, cuts, -0.22, 0.18) * drawn
    return jnp.clip(drawn, min=-reach, max=reach).astype(held_as)


def setup_inputs(seed: int = 0) -> dict:
    keys = jax.random.split(jax.random.key(seed), 12)
    obs_coords = jnp.clip(1.0 * jax.random.uniform(keys[0], (2, READ_BUF), jnp.float32) ** steps_of(keys[0], (2, READ_BUF), ((1, 32),), -0.2, 0.2), 0.0, 1.0)
    obs_codes = place_ends(jax.random.randint(keys[1], (READ_BUF,), 0, NB * C), jax.random.fold_in(keys[1], 1), 0, (NB * C) - 1).astype(jnp.int32)
    route_plan = draw_route_plan(jax.random.fold_in(keys[11], 71), 0)
    inducing_coords = jnp.clip(1.0 * jax.random.uniform(keys[3], (2, M), jnp.float32) ** steps_of(keys[3], (2, M), ((1, 8),), -0.2, 0.2), 0.0, 1.0)
    inducing_bands = place_ends(jax.random.randint(keys[4], (M,), 0, NB), jax.random.fold_in(keys[4], 1), 0, NB - 1).astype(jnp.int32)
    band_mix = normal_values(keys[5], (NB, NB), 0.4, 2.4, (), jnp.float32)
    lengthscales = jnp.clip(jnp.exp(jax.random.uniform(keys[6], (2,), jnp.float32, math.log(0.04), math.log(0.1))), 0.04, 0.1)
    class_scales = jnp.clip(jnp.exp(jax.random.uniform(keys[7], (C,), jnp.float32, math.log(0.5), math.log(2.0))), 0.5, 2.0)
    prior_factor = normal_values(keys[8], (M, MB), (16 * MB) ** -0.5, 0.046875, ((0, 256),))
    variational_chol = draw_variational_chol(jax.random.fold_in(keys[11], 71), 0)
    variational_mean = normal_values(keys[10], (C, M), 1.0, 6.0, ((1, 8),))
    return dict(obs_coords=obs_coords, obs_codes=obs_codes, route_plan=route_plan, inducing_coords=inducing_coords, inducing_bands=inducing_bands, band_mix=band_mix, lengthscales=lengthscales, class_scales=class_scales, prior_factor=prior_factor, variational_chol=variational_chol, variational_mean=variational_mean)


precise = lax.Precision.HIGHEST


def arrange(obs_coords, obs_codes, route_plan):
    capacity = obs_coords.shape[1] // N_OBS
    blocks = route_plan * 128
    send_start = (jnp.cumsum(blocks, axis=1) - blocks).astype(jnp.int32)
    recv_start = (jnp.cumsum(blocks, axis=0) - blocks).astype(jnp.int32)
    position = jnp.arange(ROWS_DEV, dtype=jnp.int32)
    sources = jnp.arange(N_OBS, dtype=jnp.int32)

    def one_device(target):
        offsets = recv_start[:, target]
        source = (jnp.sum((offsets[None, :] <= position[:, None]).astype(jnp.int32), axis=1) - 1).astype(jnp.int32)
        pick = (source[:, None] == sources[None, :]).astype(jnp.int32)
        begin_row = jnp.sum(pick * offsets[None, :], axis=1).astype(jnp.int32)
        sent_row = jnp.sum(pick * send_start[:, target][None, :], axis=1).astype(jnp.int32)
        return (source * capacity + sent_row + position - begin_row).astype(jnp.int32)

    indices = jax.vmap(one_device)(sources).reshape(-1)
    return obs_coords[:, indices], obs_codes[indices]


def cross_cov(coords, band_ids, centers, center_bands, lengthscales, coupling):
    delta_t = (coords[0][:, None] - centers[0][None, :]) / lengthscales[0]
    delta_w = (coords[1][:, None] - centers[1][None, :]) / lengthscales[1]
    kinds = jnp.arange(NB, dtype=jnp.int32)
    row_hot = (band_ids[:, None] == kinds[None, :]).astype(jnp.float32)
    col_hot = (center_bands[:, None] == kinds[None, :]).astype(jnp.float32)
    mixing = jnp.dot(jnp.dot(row_hot, coupling, precision=precise), col_hot.T, precision=precise)
    return (jnp.exp(-0.5 * (delta_t * delta_t + delta_w * delta_w)) * mixing).astype(jnp.bfloat16)


def likelihood(mean_sum, variance, class_scales):
    logits = mean_sum + 0.5 * class_scales[:, None] * variance[None, :]
    weights = jnp.exp(logits)
    chances = weights / jnp.sum(weights, axis=0, keepdims=True)
    var_slope = -0.5 * jnp.sum(chances * class_scales[:, None], axis=0)
    return chances, var_slope


def reference(obs_coords, obs_codes, route_plan, inducing_coords, inducing_bands, band_mix, lengthscales, class_scales, prior_factor, variational_chol, variational_mean):
    coords, code_ids = arrange(obs_coords, obs_codes, route_plan)
    band_ids = code_ids % NB
    labels = code_ids // NB
    coupling = jnp.eye(NB, dtype=jnp.float32) + jnp.dot(band_mix, band_mix.T, precision=precise)
    kinds = jnp.arange(NB, dtype=jnp.int32)
    row_hot = (band_ids[:, None] == kinds[None, :]).astype(jnp.float32)
    self_cov = jnp.sum(row_hot * jnp.dot(row_hot, coupling, precision=precise), axis=1)
    total_rows = coords.shape[1]
    mean_sum = jnp.zeros((C, total_rows), jnp.float32)
    var_sum = jnp.zeros((total_rows,), jnp.float32)
    whitened_all = []
    for block in range(N_IND):
        lower = block * MB
        kernel_rows = cross_cov(coords, band_ids, inducing_coords[:, lower:lower + MB], inducing_bands[lower:lower + MB], lengthscales, coupling)
        whitened = jnp.dot(kernel_rows, prior_factor[lower:lower + MB], preferred_element_type=jnp.float32)
        whitened_bf = whitened.astype(jnp.bfloat16)
        covariant = jnp.dot(whitened_bf, variational_chol[lower:lower + MB], preferred_element_type=jnp.float32)
        mean_sum = mean_sum + lax.dot_general(variational_mean[:, lower:lower + MB], whitened_bf, (((1,), (1,)), ((), ())), preferred_element_type=jnp.float32)
        var_sum = var_sum + (jnp.sum(covariant * covariant, axis=1) - jnp.sum(whitened * whitened, axis=1))
        whitened_all.append(whitened_bf)
    chances, var_slope = likelihood(mean_sum, self_cov + var_sum, class_scales)
    classes = jnp.arange(C, dtype=jnp.int32)
    mean_slope = ((labels[None, :] == classes[:, None]).astype(jnp.float32) - chances).astype(jnp.bfloat16)
    chol_grads = []
    mean_grads = []
    for block in range(N_IND):
        lower = block * MB
        whitened_bf = whitened_all[block]
        chol_block = variational_chol[lower:lower + MB]
        covariant = jnp.dot(whitened_bf, chol_block, preferred_element_type=jnp.float32)
        heavy = (2.0 * var_slope[:, None] * covariant).astype(jnp.bfloat16)
        data_term = lax.dot_general(whitened_bf, heavy, (((0,), (0,)), ((), ())), preferred_element_type=jnp.float32)
        diagonal = jnp.diagonal(chol_block).astype(jnp.float32)
        chol_grads.append(jnp.tril(data_term) - chol_block.astype(jnp.float32) + jnp.diag(1.0 / diagonal))
        mean_term = lax.dot_general(mean_slope, whitened_bf, (((1,), (0,)), ((), ())), preferred_element_type=jnp.float32)
        mean_grads.append(mean_term - variational_mean[:, lower:lower + MB].astype(jnp.float32))
    return chances, jnp.concatenate(chol_grads, axis=0), jnp.concatenate(mean_grads, axis=1)
```

```python
import functools
import math

import jax
import jax.numpy as jnp
from jax import lax
from jax.experimental import pallas as pl
from jax.experimental.pallas import tpu as pltpu
from jax.sharding import PartitionSpec as P

C = 8
NB = 6
ROWS = 2048
MB = 1024
MESH = pl.DeviceIdType.MESH
F32 = jnp.float32
BF16 = jnp.bfloat16
ROOT = math.sqrt(0.5 * math.log2(math.e))


def dot_nn(a, b):
    return jnp.dot(a, b, preferred_element_type=F32)


def dot_nt(a, b):
    return lax.dot_general(a, b, (((1,), (1,)), ((), ())), preferred_element_type=F32)


def exact_pick(hot, rows):
    return jnp.dot(hot, rows, precision=lax.Precision.HIGHEST, preferred_element_type=F32)


def kernel(
    coords_ref, codes_ref, plan_ref, centers_ref, bands_ref, mix_ref, ls_ref, scales_ref,
    w_in, l_in, m_in,
    probs_out, gchol_out, gmean_out,
    held, sendbuf, incoming, feat, crow, tab, centers_s, mpad,
    wbuf, lbuf, kbuf, abuf, atbuf, bbuf, hbuf, sq,
    stats, gathered, pieces, ms,
    gbuf, r1, s1, r2, s2, r3,
    mt0, mt1, mt2, rm1, rm2, rm3,
    route_s, route_r, agw_s, agw_r, agl_s, agl_r,
    st_s, st_r, pr_s, pr_r, p1_s, p1_r, p2_s, p2_r, p3_s, p3_r,
    m12_s, m12_r, m3_s, m3_r,
):
    me = lax.axis_index("obs")
    ib = lax.axis_index("ind")
    z = me // 4
    xh = (me // 2) % 2
    c = me % 2
    oxh = 1 - xh
    oc = 1 - c
    zp = (z + 1) % 8
    zm = (z + 7) % 8

    def at(zz, xx, cc):
        return (zz * 4 + xx * 2 + cc, ib)

    def remote(src, dst, ssem, rsem, dev):
        return pltpu.make_async_remote_copy(
            src_ref=src, dst_ref=dst, send_sem=ssem, recv_sem=rsem, device_id=dev, device_id_type=MESH
        )

    r3[...] = jnp.zeros_like(r3)

    barrier = pltpu.get_barrier_semaphore()

    def greet_obs(d, carry):
        pl.semaphore_signal(barrier, inc=1, device_id=((me + d) % 32, ib), device_id_type=MESH)
        return carry

    def greet_ind(d, carry):
        pl.semaphore_signal(barrier, inc=1, device_id=(me, (ib + d) % 8), device_id_type=MESH)
        return carry

    lax.fori_loop(1, 32, greet_obs, 0)
    lax.fori_loop(1, 8, greet_ind, 0)

    for b in range(32):
        held[0, b : b + 1, :] = coords_ref[0:1, b * 128 : b * 128 + 128]
        held[1, b : b + 1, :] = coords_ref[1:2, b * 128 : b * 128 + 128]
    plan = plan_ref[...]
    sub = lax.broadcasted_iota(jnp.int32, (32, 32), 0)
    lan = lax.broadcasted_iota(jnp.int32, (32, 32), 1)
    plan_row = jnp.sum(jnp.where(sub == me, plan, 0), axis=0, keepdims=True)
    start = jnp.sum(jnp.where(lan < sub, plan_row, 0), axis=1, keepdims=True)
    choose = (lan == start).astype(F32)
    sendbuf[:, 0, :] = exact_pick(choose, held[0])
    sendbuf[:, 1, :] = exact_pick(choose, held[1])
    sendbuf[:, 2, :] = exact_pick(choose, codes_ref[...].astype(F32))
    sendbuf[:, 3, :] = jnp.zeros((32, 128), F32)
    incoming[me] = sendbuf[me]
    wbuf[z, xh, c] = w_in[...]
    lbuf[z, xh, c] = l_in[...]

    pl.semaphore_wait(barrier, 38)

    def route_copy(d):
        peer = (me + d) % 32
        return remote(sendbuf.at[peer], incoming.at[me], route_s.at[d], route_r.at[d], (peer, ib))

    def route_start(d, carry):
        route_copy(d).start()
        return carry

    lax.fori_loop(1, 32, route_start, 0)

    class Gather:
        def __init__(self, own, buf, ss, rs):
            self.own, self.buf, self.ss, self.rs = own, buf, ss, rs

        def x_copy(self):
            b = self.buf
            return remote(self.own, b.at[z, xh, c], self.ss.at[0], self.rs.at[0], at(z, oxh, c))

        def x_recv(self):
            b = self.buf
            return remote(self.own, b.at[z, oxh, c], self.ss.at[0], self.rs.at[0], at(z, oxh, c))

        def unit(self, zz, idx, dev):
            b = self.buf
            return remote(b.at[zz, :, c], b.at[zz, :, c], self.ss.at[idx], self.rs.at[idx], dev)

        def half(self, zz, j, idx, dev):
            b = self.buf
            return remote(b.at[zz, j, c], b.at[zz, j, c], self.ss.at[idx], self.rs.at[idx], dev)

        def up(self, k):
            if k < 4:
                return self.unit((z + 8 - (k - 1)) % 8, k, at(zp, xh, c))
            return self.half((z + 5) % 8, 0, 4, at(zp, xh, c))

        def down(self, k):
            if k < 4:
                return self.unit((z + (k - 1)) % 8, 4 + k, at(zm, xh, c))
            return self.half((z + 3) % 8, 1, 8, at(zm, xh, c))

        def up_recv(self, k):
            if k < 4:
                return self.unit((z + 8 - k) % 8, k, at(zp, xh, c))
            return self.half((z + 4) % 8, 0, 4, at(zp, xh, c))

        def down_recv(self, k):
            if k < 4:
                return self.unit((z + k) % 8, 4 + k, at(zm, xh, c))
            return self.half((z + 4) % 8, 1, 8, at(zm, xh, c))

        def core(self, q):
            zz = self.core_unit(q)
            return self.unit(zz, 9 + q, at(z, xh, oc))

        def core_recv(self, q):
            b = self.buf
            zz = self.core_unit(q)
            return remote(b.at[zz, :, oc], b.at[zz, :, oc], self.ss.at[9 + q], self.rs.at[9 + q], at(z, xh, oc))

        def core_unit(self, q):
            if q == 0:
                return z
            if q == 7:
                return (z + 4) % 8
            k = (q + 1) // 2
            return (z + 8 - k) % 8 if q % 2 == 1 else (z + k) % 8

        def begin(self):
            self.x_copy().start()

        def step(self, k):
            if k == 0:
                self.x_recv().wait_recv()
                self.up(1).start()
                self.down(1).start()
                self.core(0).start()
                return
            self.up_recv(k).wait_recv()
            self.down_recv(k).wait_recv()
            if k < 4:
                self.up(k + 1).start()
                self.down(k + 1).start()
                self.core(2 * k - 1).start()
                self.core(2 * k).start()
            else:
                self.core(7).start()

        def end(self):
            for q in range(8):
                self.core_recv(q).wait_recv()

        def drain(self):
            self.x_copy().wait_send()
            for k in range(1, 5):
                self.up(k).wait_send()
                self.down(k).wait_send()
            for q in range(8):
                self.core(q).wait_send()

    gw = Gather(w_in, wbuf, agw_s, agw_r)
    gl = Gather(l_in, lbuf, agl_s, agl_r)
    gw.begin()
    gl.begin()

    ls0 = jnp.full((1, MB), ls_ref[0], F32)
    ls1 = jnp.full((1, MB), ls_ref[1], F32)
    centers_s[0:1, :] = centers_ref[0:1, :] * (ROOT / ls0)
    centers_s[1:2, :] = centers_ref[1:2, :] * (ROOT / ls1)
    kinds8 = lax.broadcasted_iota(jnp.int32, (8, 128), 0)
    for s in range(8):
        band = jnp.broadcast_to(bands_ref[s : s + 1, :], (8, 128))
        total = (band == kinds8).astype(F32)
        for i in range(NB):
            picked = jnp.zeros((8, 128), F32)
            column = jnp.zeros((8, 128), F32)
            for k in range(NB):
                picked = jnp.where(band == k, mix_ref[k, i], picked)
                column = jnp.where(kinds8 == k, mix_ref[k, i], column)
            total = total + column * picked
        high = total.astype(BF16).astype(F32)
        rest = total - high
        middle = rest.astype(BF16).astype(F32)
        low = rest - middle
        zeros = jnp.zeros((104, 128), F32)
        tab[:, s * 128 : (s + 1) * 128] = jnp.concatenate([high, middle, low, zeros], axis=0).astype(BF16)
    mpad[...] = jnp.concatenate([m_in[...].astype(F32), jnp.zeros((120, MB), F32)], axis=0).astype(BF16)

    plan_col = jnp.sum(jnp.where(lan == me, plan, 0), axis=1, keepdims=True)
    before = jnp.sum(jnp.where(sub < lan, plan_col, 0), axis=0, keepdims=True)
    sub16 = lax.broadcasted_iota(jnp.int32, (16, 32), 0)
    lan16 = lax.broadcasted_iota(jnp.int32, (16, 32), 1)
    source = jnp.sum((before <= sub16).astype(jnp.int32), axis=1, keepdims=True) - 1
    source_hot = (lan16 == source).astype(F32)

    gw.step(0)

    def route_wait(d, carry):
        src = (me + 32 - d) % 32
        remote(sendbuf.at[src], incoming.at[src], route_s.at[d], route_r.at[d], (src, ib)).wait_recv()
        return carry

    lax.fori_loop(1, 32, route_wait, 0)

    st = ROOT / jnp.full((1, 128), ls_ref[0], F32)
    sw = ROOT / jnp.full((1, 128), ls_ref[1], F32)
    code = exact_pick(source_hot, incoming[:, 2, :])
    label = jnp.zeros((16, 128), F32)
    for n in range(1, C):
        label = label + (code >= float(NB * n)).astype(F32)
    band = code - float(NB) * label
    feat[:, 0, :] = exact_pick(source_hot, incoming[:, 0, :]) * st
    feat[:, 1, :] = exact_pick(source_hot, incoming[:, 1, :]) * sw
    feat[:, 2, :] = band
    for k in range(3, 8):
        feat[:, k, :] = jnp.zeros((16, 128), F32)
    for k in range(16):
        lanes = slice((k % 2) * 128, (k % 2) * 128 + 128)
        crow[k // 2, 0:1, lanes] = label[k : k + 1, :]
        crow[k // 2, 1:2, lanes] = band[k : k + 1, :]

    lane = lax.broadcasted_iota(jnp.int32, (128, 128), 1)
    kind = (lane % 8).astype(F32)
    live = lane < 24

    def cov_block(b, carry):
        cols = jnp.transpose(feat[b])
        t = cols[:, 0:1]
        w = cols[:, 1:2]
        hot = jnp.where(live & (cols[:, 2:3] == kind), 1.0, 0.0).astype(BF16)
        rows = pl.ds(pl.multiple_of(b * 128, 128), 128)
        for s in range(4):
            lanes = slice(s * 256, s * 256 + 256)
            dt = t - centers_s[0:1, lanes]
            dw = w - centers_s[1:2, lanes]
            mixing = dot_nn(hot, tab[:, lanes])
            kbuf[rows, lanes] = (jnp.exp2(-(dt * dt + dw * dw)) * mixing).astype(BF16)
        return carry

    for part in range(4):
        lax.fori_loop(4 * part, 4 * part + 4, cov_block, 0)
        gw.step(part + 1)
    gl.step(0)
    gw.end()

    for part in range(4):
        rows = slice(part * 512, part * 512 + 512)
        for n in range(4):
            lanes = slice(n * 256, n * 256 + 256)
            a = dot_nn(kbuf[rows, :], wbuf[:, :, :, :, lanes].reshape(MB, 256))
            abuf[rows, lanes] = a.astype(BF16)
            squares = a[:, :128] * a[:, :128] + a[:, 128:] * a[:, 128:]
            if n == 0:
                sq[rows, :] = squares
            else:
                sq[rows, :] += squares
        gl.step(part + 1)
    gl.end()

    lane256 = lax.broadcasted_iota(jnp.int32, (256, 128), 1)

    def stat_copy(i):
        return remote(stats.at[i], gathered.at[ib], st_s.at[i], st_r.at[ib], (me, i))

    def b_block(i, carry):
        rows = pl.ds(pl.multiple_of(i * 256, 256), 256)
        squares = -sq[rows, :]
        for n in range(4):
            lanes = slice(n * 256, n * 256 + 256)
            deep = slice(n * 256, MB)
            lower = lbuf[2 * n :, :, :, :, lanes].reshape(MB - n * 256, 256)
            b = dot_nn(abuf[rows, deep], lower)
            bbuf[rows, lanes] = b
            squares = squares + (b[:, :128] * b[:, :128] + b[:, 128:] * b[:, 128:])
        means = dot_nt(abuf[rows, :], mpad[...])
        var = jnp.sum(squares, axis=1, keepdims=True)
        both = jnp.transpose(jnp.where(lane256 == 8, var, means))
        stats[i] = both[0:16, :]

        @pl.when(i != ib)
        def _():
            stat_copy(i).start()

        @pl.when(i == ib)
        def _():
            gathered[ib] = both[0:16, :]

        return carry

    lax.fori_loop(0, 8, b_block, 0)

    def flip(i, carry):
        rows = pl.ds(pl.multiple_of(i * 256, 256), 256)
        atbuf[:, rows] = jnp.transpose(abuf[rows, :])
        return carry

    lax.fori_loop(0, 3, flip, 0)

    def stat_wait(d, carry):
        src = (ib + d) % 8
        remote(stats.at[src], gathered.at[src], st_s.at[src], st_r.at[src], (me, src)).wait_recv()
        return carry

    lax.fori_loop(1, 8, stat_wait, 0)

    scale = jnp.zeros((8, 256), F32)
    class_ids = lax.broadcasted_iota(jnp.int32, (8, 256), 0)
    for n in range(C):
        scale = jnp.where(class_ids == n, scales_ref[n], scale)

    both = gathered[0]
    for p in range(1, 8):
        both = both + gathered[p]
    band = crow[ib, 1:2, :]
    own = jnp.zeros((1, 256), F32)
    for k in range(NB):
        value = jnp.float32(1.0)
        for i in range(NB):
            value = value + mix_ref[k, i] * mix_ref[k, i]
        own = jnp.where(band == float(k), value, own)
    logits = both[0:8, :] + 0.5 * scale * (both[8:9, :] + own)
    weights = jnp.exp(logits)
    chances = weights / jnp.sum(weights, axis=0, keepdims=True)
    pieces[ib] = chances

    def piece_copy(d):
        dev = (ib + d) % 8
        return remote(pieces.at[ib], pieces.at[ib], pr_s.at[d], pr_r.at[d], (me, dev))

    def piece_start(d, carry):
        piece_copy(d).start()
        return carry

    lax.fori_loop(1, 8, piece_start, 0)
    lax.fori_loop(3, 8, flip, 0)

    def piece_wait(d, carry):
        src = (ib + 8 - d) % 8
        remote(pieces.at[src], pieces.at[src], pr_s.at[d], pr_r.at[d], (me, src)).wait_recv()
        return carry

    lax.fori_loop(1, 8, piece_wait, 0)

    classes = class_ids.astype(F32)
    for p in range(8):
        lanes = slice(p * 256, p * 256 + 256)
        ch = pieces[p]
        probs_out[:, lanes] = ch
        slope = jnp.where(crow[p, 0:1, :] == classes, 1.0, 0.0) - ch
        ms[:, lanes] = jnp.concatenate([slope, jnp.zeros((8, 256), F32)], axis=0).astype(BF16)

    mt0[...] = dot_nn(ms[...], abuf[...])[0:8, :]
    mean1 = remote(mt0, rm1, m12_s.at[0], m12_r.at[0], at(z, xh, oc))
    mean1.start()

    def h_block(i, carry):
        rows = pl.ds(pl.multiple_of(i * 256, 256), 256)
        slope = -jnp.sum(pieces[i] * scale, axis=0, keepdims=True)
        column = jnp.transpose(jnp.broadcast_to(slope, (8, 256)))[:, 0:1]
        hbuf[rows, :] = (column * bbuf[rows, :]).astype(BF16)
        return carry

    lax.fori_loop(0, 8, h_block, 0)

    def m3_copy(d):
        return remote(mt2, rm3.at[z], m3_s.at[d], m3_r.at[d], at((z + d) % 8, xh, c))

    mean2 = remote(mt1, rm2, m12_s.at[1], m12_r.at[1], at(z, oxh, c))

    def p1_copy(n):
        lanes = pl.ds(n * 256, 256)
        return remote(
            gbuf.at[pl.ds(2 * n, 8 - 2 * n), :, oc, :, lanes],
            r1.at[pl.ds(2 * n, 8 - 2 * n), :, :, lanes],
            p1_s.at[n], p1_r.at[n], at(z, xh, oc),
        )

    def p2_copy(n):
        lanes = pl.ds(n * 256, 256)
        return remote(
            s1.at[pl.ds(2 * n, 8 - 2 * n), oxh, :, lanes],
            r2.at[pl.ds(2 * n, 8 - 2 * n), :, lanes],
            p2_s.at[n], p2_r.at[n], at(z, oxh, c),
        )

    def p3_copy(n, zz):
        lanes = pl.ds(n * 256, 256)
        return remote(
            s2.at[zz, :, lanes], r3.at[z, :, lanes], p3_s.at[n, zz], p3_r.at[n, z], at(zz, xh, c)
        )

    def stage1(n):
        lanes = slice(n * 256, n * 256 + 256)
        g = dot_nn(atbuf[n * 256 :, :], hbuf[:, lanes]).astype(BF16)
        gbuf[2 * n :, :, :, :, lanes] = g.reshape(8 - 2 * n, 2, 2, 32, 256)
        p1_copy(n).start()

    def stage2(n):
        p1_copy(n).wait_recv()
        lanes = pl.ds(n * 256, 256)

        def add(zz, carry):
            for j in range(2):
                total = gbuf[zz, j, c, :, lanes].astype(F32) + r1[zz, j, :, lanes].astype(F32)
                s1[zz, j, :, lanes] = total.astype(BF16)
            return carry

        lax.fori_loop(2 * n, 8, add, 0)
        p2_copy(n).start()

    def stage3(n):
        p2_copy(n).wait_recv()
        lanes = pl.ds(n * 256, 256)

        def add(zz, carry):
            total = s1[zz, xh, :, lanes].astype(F32) + r2[zz, :, lanes].astype(F32)
            s2[zz, :, lanes] = total.astype(BF16)

            @pl.when(zz != z)
            def _():
                p3_copy(n, zz).start()

            @pl.when(zz == z)
            def _():
                r3[z, :, lanes] = total.astype(BF16)

            return carry

        lax.fori_loop(2 * n, 8, add, 0)

    stage1(0)
    mean1.wait_recv()
    mt1[...] = mt0[...] + rm1[...]
    mean2.start()
    stage1(1)
    stage2(0)
    mean2.wait_recv()
    mt2[...] = mt1[...] + rm2[...]
    rm3[z] = mt2[...]

    def m3_start(d, carry):
        m3_copy(d).start()
        return carry

    lax.fori_loop(1, 8, m3_start, 0)
    stage1(2)
    stage2(1)
    stage3(0)
    stage1(3)
    stage2(2)
    stage3(1)
    stage2(3)
    stage3(2)
    stage3(3)

    def m3_wait(d, carry):
        src = (z + 8 - d) % 8
        remote(mt2, rm3.at[src], m3_s.at[d], m3_r.at[d], at(src, xh, c)).wait_recv()
        return carry

    lax.fori_loop(1, 8, m3_wait, 0)
    grad = rm3[0]
    for p in range(1, 8):
        grad = grad + rm3[p]
    gmean_out[...] = grad - m_in[...].astype(F32)

    def p3_wait(n):
        lanes = pl.ds(n * 256, 256)

        def one(d, carry):
            src = (z + 8 - d) % 8
            remote(
                s2.at[src, :, lanes], r3.at[src, :, lanes], p3_s.at[n, src], p3_r.at[n, src], at(src, xh, c)
            ).wait_recv()
            return carry

        @pl.when(z >= 2 * n)
        def _():
            lax.fori_loop(1, 8, one, 0)

    for n in range(4):
        p3_wait(n)
    data = r3[0].astype(F32)
    for p in range(1, 8):
        data = data + r3[p].astype(F32)
    column_ids = lax.broadcasted_iota(jnp.int32, (32, MB), 1)
    row_ids = lax.broadcasted_iota(jnp.int32, (32, MB), 0) + me * 32
    own_chol = l_in[...].astype(F32)
    on_diag = column_ids == row_ids
    diagonal = jnp.sum(jnp.where(on_diag, own_chol, 0.0), axis=1, keepdims=True)
    gchol_out[...] = (
        jnp.where(column_ids <= row_ids, data, 0.0) - own_chol + jnp.where(on_diag, 1.0 / diagonal, 0.0)
    )

    def route_drain(d, carry):
        route_copy(d).wait_send()
        return carry

    lax.fori_loop(1, 32, route_drain, 0)
    gw.drain()
    gl.drain()

    def ind_drain(d, carry):
        stat_copy((ib + d) % 8).wait_send()
        piece_copy(d).wait_send()
        m3_copy(d).wait_send()
        return carry

    lax.fori_loop(1, 8, ind_drain, 0)
    mean1.wait_send()
    mean2.wait_send()
    for n in range(4):
        p1_copy(n).wait_send()
        p2_copy(n).wait_send()

        def p3_drain(zz, carry):
            @pl.when(zz != z)
            def _():
                p3_copy(n, zz).wait_send()

            return carry

        lax.fori_loop(2 * n, 8, p3_drain, 0)


def body(
    obs_coords, obs_codes, route_plan, inducing_coords, inducing_bands, band_mix, lengthscales,
    class_scales, prior_factor, variational_chol, variational_mean,
):
    vmem = pl.BlockSpec(memory_space=pltpu.VMEM)
    smem = pl.BlockSpec(memory_space=pltpu.SMEM)
    dma = pltpu.SemaphoreType.DMA
    return pl.pallas_call(
        kernel,
        out_shape=(
            jax.ShapeDtypeStruct((C, ROWS), F32),
            jax.ShapeDtypeStruct((32, MB), F32),
            jax.ShapeDtypeStruct((C, MB), F32),
        ),
        in_specs=[vmem, vmem, vmem, vmem, vmem, smem, smem, smem, vmem, vmem, vmem],
        out_specs=(vmem, vmem, vmem),
        scratch_shapes=[
            pltpu.VMEM((2, 32, 128), F32),
            pltpu.VMEM((32, 4, 128), F32),
            pltpu.VMEM((32, 4, 128), F32),
            pltpu.VMEM((16, 8, 128), F32),
            pltpu.VMEM((8, 2, 256), F32),
            pltpu.VMEM((128, MB), BF16),
            pltpu.VMEM((2, MB), F32),
            pltpu.VMEM((128, MB), BF16),
            pltpu.VMEM((8, 2, 2, 32, MB), BF16),
            pltpu.VMEM((8, 2, 2, 32, MB), BF16),
            pltpu.VMEM((ROWS, MB), BF16),
            pltpu.VMEM((ROWS, MB), BF16),
            pltpu.VMEM((MB, ROWS), BF16),
            pltpu.VMEM((ROWS, MB), F32),
            pltpu.VMEM((ROWS, MB), BF16),
            pltpu.VMEM((ROWS, 128), F32),
            pltpu.VMEM((8, 16, 256), F32),
            pltpu.VMEM((8, 16, 256), F32),
            pltpu.VMEM((8, 8, 256), F32),
            pltpu.VMEM((16, ROWS), BF16),
            pltpu.VMEM((8, 2, 2, 32, MB), BF16),
            pltpu.VMEM((8, 2, 32, MB), BF16),
            pltpu.VMEM((8, 2, 32, MB), BF16),
            pltpu.VMEM((8, 32, MB), BF16),
            pltpu.VMEM((8, 32, MB), BF16),
            pltpu.VMEM((8, 32, MB), BF16),
            pltpu.VMEM((8, MB), F32),
            pltpu.VMEM((8, MB), F32),
            pltpu.VMEM((8, MB), F32),
            pltpu.VMEM((8, MB), F32),
            pltpu.VMEM((8, MB), F32),
            pltpu.VMEM((8, 8, MB), F32),
            dma((32,)), dma((32,)), dma((17,)), dma((17,)), dma((17,)), dma((17,)),
            dma((8,)), dma((8,)), dma((8,)), dma((8,)),
            dma((4,)), dma((4,)), dma((4,)), dma((4,)), dma((4, 8)), dma((4, 8)),
            dma((2,)), dma((2,)), dma((8,)), dma((8,)),
        ],
        compiler_params=pltpu.CompilerParams(
            collective_id=0, has_side_effects=True, vmem_limit_bytes=60 << 20
        ),
        name="elbo_step",
    )(
        obs_coords, obs_codes.reshape(32, 128), route_plan, inducing_coords,
        inducing_bands.reshape(8, 128), band_mix, lengthscales, class_scales,
        prior_factor, variational_chol, variational_mean,
    )


def solution(mesh):
    placed = (
        P(None, "obs"), P("obs"), P(), P(None, "ind"), P("ind"), P(), P(), P(),
        P(("ind", "obs"), None), P(("ind", "obs"), None), P(None, "ind"),
    )
    return jax.shard_map(
        body,
        mesh=mesh,
        in_specs=placed,
        out_specs=(P(None, "obs"), P(("ind", "obs"), None), P(None, "ind")),
        check_vma=False,
    )
```

```python
import functools
import math

import jax
import jax.numpy as jnp
from jax import lax
from jax.experimental import pallas as pl
from jax.experimental.pallas import tpu as pltpu
from jax.sharding import PartitionSpec as P

C = 8
NB = 6
ROWS = 2048
MB = 1024
MESH = pl.DeviceIdType.MESH
F32 = jnp.float32
BF16 = jnp.bfloat16
ROOT = math.sqrt(0.5 * math.log2(math.e))


def dot_nn(a, b):
    return jnp.dot(a, b, preferred_element_type=F32)


def dot_nt(a, b):
    return lax.dot_general(a, b, (((1,), (1,)), ((), ())), preferred_element_type=F32)


def exact_pick(hot, rows):
    return jnp.dot(hot, rows, precision=lax.Precision.HIGHEST, preferred_element_type=F32)


def kernel(
    coords_ref, codes_ref, plan_ref, centers_ref, bands_ref, mix_ref, ls_ref, scales_ref,
    w_in, l_in, m_in,
    probs_out, gchol_out, gmean_out,
    held, sendbuf, incoming, feat, crow, tab, centers_s, mpad,
    wbuf, lbuf, kbuf, abuf, atbuf, bbuf, hbuf, sq,
    terms, ms,
    gbuf, r1, s1, r2, s2, r3,
    mt0, mt1, mt2, rm1, rm2, rm3, quarters,
    route_s, route_r, agw_s, agw_r, agl_s, agl_r,
    st_s, st_r, p1_s, p1_r, p2_s, p2_r, p3_s, p3_r,
    m12_s, m12_r, m3_s, m3_r, m4_s, m4_r,
):
    me = lax.axis_index("obs")
    ib = lax.axis_index("ind")
    z = me // 4
    xh = (me // 2) % 2
    c = me % 2
    oxh = 1 - xh
    oc = 1 - c
    zp = (z + 1) % 8
    zm = (z + 7) % 8

    def at(zz, xx, cc):
        return (zz * 4 + xx * 2 + cc, ib)

    def remote(src, dst, ssem, rsem, dev):
        return pltpu.make_async_remote_copy(
            src_ref=src, dst_ref=dst, send_sem=ssem, recv_sem=rsem, device_id=dev, device_id_type=MESH
        )

    r3[...] = jnp.zeros_like(r3)

    barrier = pltpu.get_barrier_semaphore()

    def greet_obs(d, carry):
        pl.semaphore_signal(barrier, inc=1, device_id=((me + d) % 32, ib), device_id_type=MESH)
        return carry

    def greet_ind(d, carry):
        pl.semaphore_signal(barrier, inc=1, device_id=(me, (ib + d) % 8), device_id_type=MESH)
        return carry

    lax.fori_loop(1, 32, greet_obs, 0)
    lax.fori_loop(1, 8, greet_ind, 0)

    for b in range(32):
        held[0, b : b + 1, :] = coords_ref[0:1, b * 128 : b * 128 + 128]
        held[1, b : b + 1, :] = coords_ref[1:2, b * 128 : b * 128 + 128]
    plan = plan_ref[...]
    sub = lax.broadcasted_iota(jnp.int32, (32, 32), 0)
    lan = lax.broadcasted_iota(jnp.int32, (32, 32), 1)
    plan_row = jnp.sum(jnp.where(sub == me, plan, 0), axis=0, keepdims=True)
    start = jnp.sum(jnp.where(lan < sub, plan_row, 0), axis=1, keepdims=True)
    choose = (lan == start).astype(F32)
    sendbuf[:, 0, :] = exact_pick(choose, held[0])
    sendbuf[:, 1, :] = exact_pick(choose, held[1])
    sendbuf[:, 2, :] = exact_pick(choose, codes_ref[...].astype(F32))
    sendbuf[:, 3, :] = jnp.zeros((32, 128), F32)
    incoming[me] = sendbuf[me]
    wbuf[z, xh, c] = w_in[...]
    lbuf[z, xh, c] = l_in[...]

    pl.semaphore_wait(barrier, 38)

    def route_copy(d):
        peer = (me + d) % 32
        return remote(sendbuf.at[peer], incoming.at[me], route_s.at[d], route_r.at[d], (peer, ib))

    def route_start(d, carry):
        route_copy(d).start()
        return carry

    lax.fori_loop(1, 32, route_start, 0)

    class Gather:
        def __init__(self, own, buf, ss, rs, triangular):
            self.own, self.buf, self.ss, self.rs, self.triangular = own, buf, ss, rs, triangular

        def widths(self, zz, fn):
            if not self.triangular:
                fn(slice(None))
                return
            for v in range(4):

                @pl.when(zz // 2 == v)
                def _():
                    fn(pl.ds(0, (v + 1) * 256))

        def shard(self, zz, j, cc, lanes):
            if self.triangular:
                return self.buf.at[zz, j, cc, :, lanes]
            return self.buf.at[zz, j, cc]

        def go(self, op, zz, j, cc, idx, dev, mine=False):
            def fn(lanes):
                dst = self.shard(zz, j, cc, lanes)
                src = dst
                if mine:
                    src = self.own.at[:, lanes] if self.triangular else self.own
                copy = remote(src, dst, self.ss.at[idx], self.rs.at[idx], dev)
                getattr(copy, op)()

            self.widths(zz, fn)

        def half(self, stream):
            return xh if stream == 0 else oxh

        def up(self, op, stream, k):
            zz = (z + 8 - (k - 1)) % 8
            self.go(op, zz, self.half(stream), c, 7 * stream + k, at(zp, xh, c), stream == 0 and k == 1)

        def down(self, op, stream, k):
            zz = (z + k - 1) % 8
            self.go(op, zz, self.half(stream), c, 7 * stream + 3 + k, at(zm, xh, c), stream == 0 and k == 1)

        def fourth(self, op, stream):
            j = self.half(stream)
            self.go(op, (z + 5 + 6 * j) % 8, j, c, 7 * stream + 7, at((z + 1 + 6 * j) % 8, xh, c))

        def unit(self, q):
            return (z + (0, 7, 6, 5, 1, 2, 3, 4)[q]) % 8

        def core(self, op, stream, q):
            mine = stream == 0 and q == 0
            self.go(op, self.unit(q), self.half(stream), c, 15 + 8 * stream + q, at(z, xh, oc), mine)

        def x_copy(self, op):
            self.go(op, z, xh, c, 0, at(z, oxh, c), True)

        def begin(self):
            self.up("start", 0, 1)
            self.down("start", 0, 1)
            self.x_copy("start")
            self.core("start", 0, 0)

        def step(self, stream, k):
            j = self.half(stream)
            if k == 0:
                self.go("wait_recv", z, oxh, c, 0, at(z, oxh, c))
                self.up("start", 1, 1)
                self.down("start", 1, 1)
                self.core("start", 1, 0)
                return
            if k == 4:
                self.go("wait_recv", (z + 4) % 8, j, c, 7 * stream + 7, at(zp, xh, c))
                self.core("start", stream, 7)
                return
            self.go("wait_recv", (z + 8 - k) % 8, j, c, 7 * stream + k, at(zp, xh, c))
            if k < 3:
                self.up("start", stream, k + 1)
            self.go("wait_recv", (z + k) % 8, j, c, 7 * stream + 3 + k, at(zm, xh, c))
            if k < 3:
                self.down("start", stream, k + 1)
            else:
                self.fourth("start", stream)
            self.core("start", stream, k)
            self.core("start", stream, 3 + k)

        def end(self):
            for stream in range(2):
                for q in range(8):
                    self.go("wait_recv", self.unit(q), self.half(stream), oc, 15 + 8 * stream + q, at(z, xh, oc))

        def drain(self):
            self.x_copy("wait_send")
            for stream in range(2):
                for k in range(1, 4):
                    self.up("wait_send", stream, k)
                    self.down("wait_send", stream, k)
                self.fourth("wait_send", stream)
                for q in range(8):
                    self.core("wait_send", stream, q)

    gw = Gather(w_in, wbuf, agw_s, agw_r, False)
    gl = Gather(l_in, lbuf, agl_s, agl_r, True)
    gw.begin()

    ls0 = jnp.full((1, MB), ls_ref[0], F32)
    ls1 = jnp.full((1, MB), ls_ref[1], F32)
    centers_s[0:1, :] = centers_ref[0:1, :] * (ROOT / ls0)
    centers_s[1:2, :] = centers_ref[1:2, :] * (ROOT / ls1)
    kinds8 = lax.broadcasted_iota(jnp.int32, (8, 128), 0)
    for s in range(8):
        band = jnp.broadcast_to(bands_ref[s : s + 1, :], (8, 128))
        total = (band == kinds8).astype(F32)
        for i in range(NB):
            picked = jnp.zeros((8, 128), F32)
            column = jnp.zeros((8, 128), F32)
            for k in range(NB):
                picked = jnp.where(band == k, mix_ref[k, i], picked)
                column = jnp.where(kinds8 == k, mix_ref[k, i], column)
            total = total + column * picked
        high = total.astype(BF16).astype(F32)
        rest = total - high
        middle = rest.astype(BF16).astype(F32)
        low = rest - middle
        zeros = jnp.zeros((104, 128), F32)
        tab[:, s * 128 : (s + 1) * 128] = jnp.concatenate([high, middle, low, zeros], axis=0).astype(BF16)
    mpad[...] = jnp.concatenate([m_in[...].astype(F32), jnp.zeros((120, MB), F32)], axis=0).astype(BF16)

    plan_col = jnp.sum(jnp.where(lan == me, plan, 0), axis=1, keepdims=True)
    before = jnp.sum(jnp.where(sub < lan, plan_col, 0), axis=0, keepdims=True)
    sub16 = lax.broadcasted_iota(jnp.int32, (16, 32), 0)
    lan16 = lax.broadcasted_iota(jnp.int32, (16, 32), 1)
    source = jnp.sum((before <= sub16).astype(jnp.int32), axis=1, keepdims=True) - 1
    source_hot = (lan16 == source).astype(F32)

    gw.step(0, 1)
    gw.step(1, 0)
    gl.begin()

    def route_wait(d, carry):
        src = (me + 32 - d) % 32
        remote(sendbuf.at[src], incoming.at[src], route_s.at[d], route_r.at[d], (src, ib)).wait_recv()
        return carry

    lax.fori_loop(1, 32, route_wait, 0)

    st = ROOT / jnp.full((1, 128), ls_ref[0], F32)
    sw = ROOT / jnp.full((1, 128), ls_ref[1], F32)
    code = exact_pick(source_hot, incoming[:, 2, :])
    label = jnp.zeros((16, 128), F32)
    for n in range(1, C):
        label = label + (code >= float(NB * n)).astype(F32)
    band = code - float(NB) * label
    feat[:, 0, :] = exact_pick(source_hot, incoming[:, 0, :]) * st
    feat[:, 1, :] = exact_pick(source_hot, incoming[:, 1, :]) * sw
    feat[:, 2, :] = band
    for k in range(3, 8):
        feat[:, k, :] = jnp.zeros((16, 128), F32)
    for k in range(16):
        lanes = slice((k % 2) * 128, (k % 2) * 128 + 128)
        crow[k // 2, 0:1, lanes] = label[k : k + 1, :]
        crow[k // 2, 1:2, lanes] = band[k : k + 1, :]

    lane = lax.broadcasted_iota(jnp.int32, (128, 128), 1)
    kind = (lane % 8).astype(F32)
    live = lane < 24

    def cov_block(b, carry):
        cols = jnp.transpose(feat[b])
        t = cols[:, 0:1]
        w = cols[:, 1:2]
        hot = jnp.where(live & (cols[:, 2:3] == kind), 1.0, 0.0).astype(BF16)
        rows = pl.ds(pl.multiple_of(b * 128, 128), 128)
        for s in range(4):
            lanes = slice(s * 256, s * 256 + 256)
            dt = t - centers_s[0:1, lanes]
            dw = w - centers_s[1:2, lanes]
            mixing = dot_nn(hot, tab[:, lanes])
            kbuf[rows, lanes] = (jnp.exp2(-(dt * dt + dw * dw)) * mixing).astype(BF16)
        return carry

    order = (
        (2, ((gw, 0, 2),)),
        (4, ((gw, 1, 1),)),
        (6, ((gl, 0, 1), (gl, 1, 0))),
        (8, ((gw, 0, 3),)),
        (10, ((gw, 1, 2), (gl, 0, 2))),
        (12, ((gw, 0, 4), (gl, 1, 1))),
        (16, ((gw, 1, 3), (gl, 0, 3), (gw, 1, 4))),
    )
    done = 0
    for upto, events in order:
        lax.fori_loop(done, upto, cov_block, 0)
        done = upto
        for g, stream, k in events:
            g.step(stream, k)
    gw.end()

    turn = 0
    plan_l = {3: (1, 2), 6: (0, 4), 9: (1, 3), 13: (1, 4)}
    for part in range(4):
        rows = slice(part * 512, part * 512 + 512)
        for n in range(4):
            lanes = slice(n * 256, n * 256 + 256)
            a = dot_nn(kbuf[rows, :], wbuf[:, :, :, :, lanes].reshape(MB, 256))
            abuf[rows, lanes] = a.astype(BF16)
            squares = a[:, :128] * a[:, :128] + a[:, 128:] * a[:, 128:]
            if n == 0:
                sq[rows, :] = squares
            else:
                sq[rows, :] += squares
            if turn in plan_l:
                gl.step(*plan_l[turn])
            turn += 1
    gl.end()

    lane256 = lax.broadcasted_iota(jnp.int32, (256, 128), 1)
    class_ids = lax.broadcasted_iota(jnp.int32, (8, 256), 0)
    scale = jnp.zeros((8, 256), F32)
    for n in range(C):
        scale = jnp.where(class_ids == n, scales_ref[n], scale)

    def term_copy(i, d):
        slot = terms.at[ib, i]
        return remote(slot, slot, st_s.at[i, d], st_r.at[i, d], (me, (ib + d) % 8))

    def b_block(i, carry):
        rows = pl.ds(pl.multiple_of(i * 256, 256), 256)
        squares = -sq[rows, :]
        for n in range(4):
            lanes = slice(n * 256, n * 256 + 256)
            deep = slice(n * 256, MB)
            lower = lbuf[2 * n :, :, :, :, lanes].reshape(MB - n * 256, 256)
            b = dot_nn(abuf[rows, deep], lower)
            bbuf[rows, lanes] = b
            squares = squares + (b[:, :128] * b[:, :128] + b[:, 128:] * b[:, 128:])
        means = dot_nt(abuf[rows, :], mpad[...])
        var = jnp.sum(squares, axis=1, keepdims=True)
        both = jnp.transpose(jnp.where(lane256 == 8, var, means))
        terms[ib, i] = both[0:8, :] + 0.5 * scale * both[8:9, :]

        def send(d, carry):
            term_copy(i, d).start()
            return carry

        lax.fori_loop(1, 8, send, 0)
        return carry

    lax.fori_loop(0, 8, b_block, 0)

    def flip(i, carry):
        rows = pl.ds(pl.multiple_of(i * 256, 256), 256)
        atbuf[:, rows] = jnp.transpose(abuf[rows, :])
        return carry

    lax.fori_loop(0, 8, flip, 0)

    def term_wait(i, carry):
        def one(d, carry):
            src = (ib + 8 - d) % 8
            slot = terms.at[src, i]
            remote(slot, slot, st_s.at[i, d], st_r.at[i, d], (me, src)).wait_recv()
            return carry

        return lax.fori_loop(1, 8, one, carry)

    values = []
    for k in range(NB):
        value = jnp.float32(1.0)
        for i in range(NB):
            value = value + mix_ref[k, i] * mix_ref[k, i]
        values.append(value)
    classes = class_ids.astype(F32)

    def likelihood(p):
        lanes = slice(p * 256, p * 256 + 256)
        logits = terms[0, p]
        for q in range(1, 8):
            logits = logits + terms[q, p]
        band = crow[p, 1:2, :]
        own = jnp.zeros((1, 256), F32)
        for k in range(NB):
            own = jnp.where(band == float(k), values[k], own)
        weights = jnp.exp(logits + 0.5 * scale * own)
        ch = weights / jnp.sum(weights, axis=0, keepdims=True)
        probs_out[:, lanes] = ch
        slope = jnp.where(crow[p, 0:1, :] == classes, 1.0, 0.0) - ch
        ms[:, lanes] = jnp.concatenate([slope, jnp.zeros((8, 256), F32)], axis=0).astype(BF16)
        slope = -jnp.sum(ch * scale, axis=0, keepdims=True)
        column = jnp.transpose(jnp.broadcast_to(slope, (8, 256)))[:, 0:1]
        rows = slice(p * 256, p * 256 + 256)
        hbuf[rows, :] = (column * bbuf[rows, :]).astype(BF16)

    lax.fori_loop(0, 4, term_wait, 0)
    for p in range(4):
        likelihood(p)
    mt0[...] = dot_nn(ms[:, 0:1024], abuf[0:1024, :])[0:8, :]
    for n in range(4):
        lanes = slice(n * 256, n * 256 + 256)
        for lo in range(n * 256, MB, 512):
            hi = min(lo + 512, MB)
            bbuf[lo:hi, lanes] = dot_nn(atbuf[lo:hi, 0:1024], hbuf[0:1024, lanes])
    lax.fori_loop(4, 8, term_wait, 0)
    for p in range(4, 8):
        likelihood(p)

    mt0[...] += dot_nn(ms[:, 1024:2048], abuf[1024:2048, :])[0:8, :]
    mean1 = remote(mt0, rm1, m12_s.at[0], m12_r.at[0], at(z, xh, oc))
    mean1.start()

    colour = xh * 2 + c

    def m3_copy(d):
        return remote(mt2.at[colour], rm3.at[z], m3_s.at[d], m3_r.at[d], at((z + d) % 8, xh, c))

    def m4_copy(k):
        dev = (at(z, xh, oc), at(z, oxh, c), at(z, oxh, oc))[k]
        return remote(quarters.at[colour], quarters.at[colour], m4_s.at[k], m4_r.at[k], dev)

    def m4_recv(k):
        src = (xh * 2 + oc, oxh * 2 + c, oxh * 2 + oc)[k]
        return remote(quarters.at[src], quarters.at[src], m4_s.at[k], m4_r.at[k], at(z, xh, oc))

    mean2 = remote(mt1, rm2, m12_s.at[1], m12_r.at[1], at(z, oxh, c))

    def p1_copy(n):
        lanes = pl.ds(n * 256, 256)
        return remote(
            gbuf.at[pl.ds(2 * n, 8 - 2 * n), :, oc, :, lanes],
            r1.at[pl.ds(2 * n, 8 - 2 * n), :, :, lanes],
            p1_s.at[n], p1_r.at[n], at(z, xh, oc),
        )

    def p2_copy(n):
        lanes = pl.ds(n * 256, 256)
        return remote(
            s1.at[pl.ds(2 * n, 8 - 2 * n), oxh, :, lanes],
            r2.at[pl.ds(2 * n, 8 - 2 * n), :, lanes],
            p2_s.at[n], p2_r.at[n], at(z, oxh, c),
        )

    def p3_copy(n, zz):
        lanes = pl.ds(n * 256, 256)
        return remote(
            s2.at[zz, :, lanes], r3.at[z, :, lanes], p3_s.at[n, zz], p3_r.at[n, z], at(zz, xh, c)
        )

    def stage1(n):
        lanes = slice(n * 256, n * 256 + 256)
        for lo in range(n * 256, MB, 512):
            hi = min(lo + 512, MB)
            g = dot_nn(atbuf[lo:hi, 1024:2048], hbuf[1024:2048, lanes])
            g = (g + bbuf[lo:hi, lanes]).astype(BF16)
            gbuf[lo // 128 : hi // 128, :, :, :, lanes] = g.reshape((hi - lo) // 128, 2, 2, 32, 256)
        p1_copy(n).start()

    def stage2(n):
        p1_copy(n).wait_recv()
        lanes = pl.ds(n * 256, 256)

        def add(zz, carry):
            for j in range(2):
                total = gbuf[zz, j, c, :, lanes].astype(F32) + r1[zz, j, :, lanes].astype(F32)
                s1[zz, j, :, lanes] = total.astype(BF16)
            return carry

        lax.fori_loop(2 * n, 8, add, 0)
        p2_copy(n).start()

    def stage3(n):
        p2_copy(n).wait_recv()
        lanes = pl.ds(n * 256, 256)

        def add(zz, carry):
            total = s1[zz, xh, :, lanes].astype(F32) + r2[zz, :, lanes].astype(F32)
            s2[zz, :, lanes] = total.astype(BF16)

            @pl.when(zz != z)
            def _():
                p3_copy(n, zz).start()

            @pl.when(zz == z)
            def _():
                r3[z, :, lanes] = total.astype(BF16)

            return carry

        lax.fori_loop(2 * n, 8, add, 0)

    def m3_start(d, carry):
        m3_copy(d).start()
        return carry

    def m3_wait(d, carry):
        src = (z + 8 - d) % 8
        remote(mt2.at[colour], rm3.at[src], m3_s.at[d], m3_r.at[d], at(src, xh, c)).wait_recv()
        return carry

    stage1(0)
    mean1.wait_recv()
    mt1[...] = mt0[...] + rm1[...]
    mean2.start()
    stage1(1)
    stage2(0)
    stage1(2)
    stage2(1)
    stage1(3)
    stage2(2)
    stage2(3)
    mean2.wait_recv()
    for k in range(4):
        lanes = slice(k * 256, k * 256 + 256)
        mt2[k] = mt1[:, lanes] + rm2[:, lanes]
    rm3[z] = mt2[colour]
    lax.fori_loop(1, 8, m3_start, 0)
    stage3(0)
    stage3(1)
    lax.fori_loop(1, 8, m3_wait, 0)
    grad = rm3[0]
    for p in range(1, 8):
        grad = grad + rm3[p]
    quarters[colour] = grad
    for k in range(3):
        m4_copy(k).start()
    stage3(2)
    stage3(3)
    for k in range(3):
        m4_recv(k).wait_recv()
    for k in range(4):
        lanes = slice(k * 256, k * 256 + 256)
        gmean_out[:, lanes] = quarters[k] - m_in[:, lanes].astype(F32)

    def p3_wait(n):
        lanes = pl.ds(n * 256, 256)

        def one(d, carry):
            src = (z + 8 - d) % 8
            remote(
                s2.at[src, :, lanes], r3.at[src, :, lanes], p3_s.at[n, src], p3_r.at[n, src], at(src, xh, c)
            ).wait_recv()
            return carry

        @pl.when(z >= 2 * n)
        def _():
            lax.fori_loop(1, 8, one, 0)

    for n in range(4):
        p3_wait(n)
    data = r3[0].astype(F32)
    for p in range(1, 8):
        data = data + r3[p].astype(F32)
    column_ids = lax.broadcasted_iota(jnp.int32, (32, MB), 1)
    row_ids = lax.broadcasted_iota(jnp.int32, (32, MB), 0) + me * 32
    own_chol = l_in[...].astype(F32)
    on_diag = column_ids == row_ids
    diagonal = jnp.sum(jnp.where(on_diag, own_chol, 0.0), axis=1, keepdims=True)
    gchol_out[...] = (
        jnp.where(column_ids <= row_ids, data, 0.0) - own_chol + jnp.where(on_diag, 1.0 / diagonal, 0.0)
    )

    def route_drain(d, carry):
        route_copy(d).wait_send()
        return carry

    lax.fori_loop(1, 32, route_drain, 0)
    gw.drain()
    gl.drain()

    def ind_drain(d, carry):
        for i in range(8):
            term_copy(i, d).wait_send()
        m3_copy(d).wait_send()
        return carry

    lax.fori_loop(1, 8, ind_drain, 0)
    mean1.wait_send()
    mean2.wait_send()
    for k in range(3):
        m4_copy(k).wait_send()
    for n in range(4):
        p1_copy(n).wait_send()
        p2_copy(n).wait_send()

        def p3_drain(zz, carry):
            @pl.when(zz != z)
            def _():
                p3_copy(n, zz).wait_send()

            return carry

        lax.fori_loop(2 * n, 8, p3_drain, 0)


def body(
    obs_coords, obs_codes, route_plan, inducing_coords, inducing_bands, band_mix, lengthscales,
    class_scales, prior_factor, variational_chol, variational_mean,
):
    vmem = pl.BlockSpec(memory_space=pltpu.VMEM)
    smem = pl.BlockSpec(memory_space=pltpu.SMEM)
    dma = pltpu.SemaphoreType.DMA
    return pl.pallas_call(
        kernel,
        out_shape=(
            jax.ShapeDtypeStruct((C, ROWS), F32),
            jax.ShapeDtypeStruct((32, MB), F32),
            jax.ShapeDtypeStruct((C, MB), F32),
        ),
        in_specs=[vmem, vmem, vmem, vmem, vmem, smem, smem, smem, vmem, vmem, vmem],
        out_specs=(vmem, vmem, vmem),
        scratch_shapes=[
            pltpu.VMEM((2, 32, 128), F32),
            pltpu.VMEM((32, 4, 128), F32),
            pltpu.VMEM((32, 4, 128), F32),
            pltpu.VMEM((16, 8, 128), F32),
            pltpu.VMEM((8, 2, 256), F32),
            pltpu.VMEM((128, MB), BF16),
            pltpu.VMEM((2, MB), F32),
            pltpu.VMEM((128, MB), BF16),
            pltpu.VMEM((8, 2, 2, 32, MB), BF16),
            pltpu.VMEM((8, 2, 2, 32, MB), BF16),
            pltpu.VMEM((ROWS, MB), BF16),
            pltpu.VMEM((ROWS, MB), BF16),
            pltpu.VMEM((MB, ROWS), BF16),
            pltpu.VMEM((ROWS, MB), F32),
            pltpu.VMEM((ROWS, MB), BF16),
            pltpu.VMEM((ROWS, 128), F32),
            pltpu.VMEM((8, 8, 8, 256), F32),
            pltpu.VMEM((16, ROWS), BF16),
            pltpu.VMEM((8, 2, 2, 32, MB), BF16),
            pltpu.VMEM((8, 2, 32, MB), BF16),
            pltpu.VMEM((8, 2, 32, MB), BF16),
            pltpu.VMEM((8, 32, MB), BF16),
            pltpu.VMEM((8, 32, MB), BF16),
            pltpu.VMEM((8, 32, MB), BF16),
            pltpu.VMEM((8, MB), F32),
            pltpu.VMEM((8, MB), F32),
            pltpu.VMEM((4, 8, 256), F32),
            pltpu.VMEM((8, MB), F32),
            pltpu.VMEM((8, MB), F32),
            pltpu.VMEM((8, 8, 256), F32),
            pltpu.VMEM((4, 8, 256), F32),
            dma((32,)), dma((32,)), dma((31,)), dma((31,)), dma((31,)), dma((31,)),
            dma((8, 8)), dma((8, 8)),
            dma((4,)), dma((4,)), dma((4,)), dma((4,)), dma((4, 8)), dma((4, 8)),
            dma((2,)), dma((2,)), dma((8,)), dma((8,)), dma((3,)), dma((3,)),
        ],
        compiler_params=pltpu.CompilerParams(
            collective_id=0, has_side_effects=True, vmem_limit_bytes=60 << 20
        ),
        name="elbo_step",
    )(
        obs_coords, obs_codes.reshape(32, 128), route_plan, inducing_coords,
        inducing_bands.reshape(8, 128), band_mix, lengthscales, class_scales,
        prior_factor, variational_chol, variational_mean,
    )


def solution(mesh):
    placed = (
        P(None, "obs"), P("obs"), P(), P(None, "ind"), P("ind"), P(), P(), P(),
        P(("ind", "obs"), None), P(("ind", "obs"), None), P(None, "ind"),
    )
    return jax.shard_map(
        body,
        mesh=mesh,
        in_specs=placed,
        out_specs=(P(None, "obs"), P(("ind", "obs"), None), P(None, "ind")),
        check_vma=False,
    )
```

```python
import functools
import math

import jax
import jax.numpy as jnp
from jax import lax
from jax.experimental import pallas as pl
from jax.experimental.pallas import tpu as pltpu
from jax.sharding import PartitionSpec as P

C = 8
NB = 6
ROWS = 2048
MB = 1024
MESH = pl.DeviceIdType.MESH
F32 = jnp.float32
BF16 = jnp.bfloat16
ROOT = math.sqrt(0.5 * math.log2(math.e))


def dot_nn(a, b):
    return jnp.dot(a, b, preferred_element_type=F32)


def dot_nt(a, b):
    return lax.dot_general(a, b, (((1,), (1,)), ((), ())), preferred_element_type=F32)


def exact_pick(hot, rows):
    return jnp.dot(hot, rows, precision=lax.Precision.HIGHEST, preferred_element_type=F32)


def kernel(
    coords_in, codes_in, plan_in, centers_in, bands_in, mix_ref, ls_ref, scales_ref,
    w_in, l_in, m_any,
    probs_out, gchol_out, gmean_out,
    coords_ref, codes_ref, plan_ref, centers_ref, bands_ref, m_in, load_sem,
    held, sendbuf, incoming, feat, crow, tab, centers_s, mpad,
    wbuf, lbuf, kbuf, abuf, atbuf, bbuf, hbuf, sq,
    terms, ms,
    gbuf, r1, s1, r2, s2, r3,
    mt0, mt1, mt2, rm1, rm2, rm3, quarters,
    route_s, route_r, agw_s, agw_r, agl_s, agl_r,
    st_s, st_r, p1_s, p1_r, p2_s, p2_r, p3_s, p3_r,
    m12_s, m12_r, m3_s, m3_r, m4_s, m4_r,
):
    me = lax.axis_index("obs")
    ib = lax.axis_index("ind")
    z = me // 4
    xh = (me // 2) % 2
    c = me % 2
    oxh = 1 - xh
    oc = 1 - c
    zp = (z + 1) % 8
    zm = (z + 7) % 8

    def at(zz, xx, cc):
        return (zz * 4 + xx * 2 + cc, ib)

    def remote(src, dst, ssem, rsem, dev):
        return pltpu.make_async_remote_copy(
            src_ref=src, dst_ref=dst, send_sem=ssem, recv_sem=rsem, device_id=dev, device_id_type=MESH
        )

    loads = [
        pltpu.make_async_copy(src, dst, load_sem.at[k])
        for k, (src, dst) in enumerate((
            (coords_in, coords_ref), (codes_in, codes_ref), (plan_in, plan_ref),
            (w_in, wbuf.at[z, xh, c]), (l_in, lbuf.at[z, xh, c]),
            (centers_in, centers_ref), (bands_in, bands_ref), (m_any, m_in),
        ))
    ]
    for copy in loads:
        copy.start()
    r3[...] = jnp.zeros_like(r3)

    barrier = pltpu.get_barrier_semaphore()

    def greet_obs(d, carry):
        pl.semaphore_signal(barrier, inc=1, device_id=((me + d) % 32, ib), device_id_type=MESH)
        return carry

    def greet_ind(d, carry):
        pl.semaphore_signal(barrier, inc=1, device_id=(me, (ib + d) % 8), device_id_type=MESH)
        return carry

    lax.fori_loop(1, 32, greet_obs, 0)
    lax.fori_loop(1, 8, greet_ind, 0)

    for copy in loads:
        copy.wait()
    for b in range(32):
        held[0, b : b + 1, :] = coords_ref[0:1, b * 128 : b * 128 + 128]
        held[1, b : b + 1, :] = coords_ref[1:2, b * 128 : b * 128 + 128]
    plan = plan_ref[...]
    sub = lax.broadcasted_iota(jnp.int32, (32, 32), 0)
    lan = lax.broadcasted_iota(jnp.int32, (32, 32), 1)
    plan_row = jnp.sum(jnp.where(sub == me, plan, 0), axis=0, keepdims=True)
    start = jnp.sum(jnp.where(lan < sub, plan_row, 0), axis=1, keepdims=True)
    choose = (lan == start).astype(F32)
    sendbuf[:, 0, :] = exact_pick(choose, held[0])
    sendbuf[:, 1, :] = exact_pick(choose, held[1])
    sendbuf[:, 2, :] = exact_pick(choose, codes_ref[...].astype(F32))
    sendbuf[:, 3, :] = jnp.zeros((32, 128), F32)
    incoming[me] = sendbuf[me]

    pl.semaphore_wait(barrier, 38)

    def route_copy(d):
        peer = (me + d) % 32
        return remote(sendbuf.at[peer], incoming.at[me], route_s, route_r, (peer, ib))

    def route_start(d, carry):
        route_copy(d).start()
        return carry

    lax.fori_loop(1, 32, route_start, 0)

    class Gather:
        def __init__(self, buf, ss, rs, triangular):
            self.buf, self.ss, self.rs, self.triangular = buf, ss, rs, triangular

        def widths(self, zz, fn):
            if not self.triangular:
                fn(slice(None))
                return
            for v in range(4):

                @pl.when(zz // 2 == v)
                def _():
                    fn(pl.ds(0, (v + 1) * 256))

        def go(self, op, q, j, cc, idx, dev):
            zz = self.unit(q)

            def fn(lanes):
                slot = self.buf.at[zz, j, cc, :, lanes] if self.triangular else self.buf.at[zz, j, cc]
                getattr(remote(slot, slot, self.ss.at[q], self.rs.at[idx], dev), op)()

            self.widths(zz, fn)

        def unit(self, q):
            return (z + (0, 7, 6, 5, 1, 2, 3, 4)[q]) % 8

        def half(self, stream):
            return xh if stream == 0 else oxh

        def along(self, op, stream, q, hops, to):
            idx = 7 * stream + to
            self.go(op, q, self.half(stream), c, idx, at((z + 8 + hops) % 8, xh, c))

        def fourth(self, op):
            for j in range(2):

                @pl.when(xh == j)
                def _():
                    self.along(op, 0, 3 + 3 * j, 1 - 2 * j, 7)

        def core(self, op, stream, q):
            self.go(op, q, self.half(stream), c, 15, at(z, xh, oc))

        def across(self, op, q):
            self.go(op, q, xh, c, 7 + q if q else 0, at(z, oxh, c))

        def wait(self, stream, q):
            idx = 7 * stream + q if q else 0
            self.go("wait_recv", q, self.half(stream), c, idx, at(z, oxh, c))

        def begin(self):
            self.along("start", 0, 0, 1, 1)
            self.along("start", 0, 0, -1, 4)
            self.across("start", 0)
            self.core("start", 0, 0)

        def step(self, stream, k):
            if k == 0:
                self.wait(1, 0)
                self.along("start", 1, 0, 1, 1)
                self.along("start", 1, 0, -1, 4)
                self.core("start", 1, 0)
                return
            if k == 4:
                self.wait(stream, 7)
                if stream == 0:
                    self.across("start", 7)
                self.core("start", stream, 7)
                return
            relay = k < 3 - stream
            self.wait(stream, k)
            if relay:
                self.along("start", stream, k, 1, k + 1)
            self.wait(stream, 3 + k)
            if relay:
                self.along("start", stream, 3 + k, -1, 4 + k)
            if stream == 0 and k == 3:
                self.fourth("start")
                self.across("start", 3)
                self.across("start", 6)
            self.core("start", stream, k)
            self.core("start", stream, 3 + k)

        def end(self):
            rows = pl.ds(0, 320 if self.triangular else 512)
            remote(kbuf.at[rows], abuf.at[rows], self.ss.at[0], self.rs.at[15], at(z, xh, oc)).wait_recv()

        def drain(self):
            for q in range(8):
                many = (7, 4, 3, 3, 4, 3, 3, 3)[q]

                def settle(count):
                    def fn(lanes):
                        rows = pl.ds(0, 32 * count)
                        remote(
                            kbuf.at[rows, lanes], abuf.at[rows, lanes], self.ss.at[q], self.rs.at[15], at(z, xh, oc)
                        ).wait_send()

                    self.widths(self.unit(q), fn)

                if q in (3, 6):
                    pl.when(xh == (q - 3) // 3)(functools.partial(settle, many + 1))
                    pl.when(xh != (q - 3) // 3)(functools.partial(settle, many))
                else:
                    settle(many)

    gw = Gather(wbuf, agw_s, agw_r, False)
    gl = Gather(lbuf, agl_s, agl_r, True)
    gw.begin()

    ls0 = jnp.full((1, MB), ls_ref[0], F32)
    ls1 = jnp.full((1, MB), ls_ref[1], F32)
    centers_s[0:1, :] = centers_ref[0:1, :] * (ROOT / ls0)
    centers_s[1:2, :] = centers_ref[1:2, :] * (ROOT / ls1)
    kinds8 = lax.broadcasted_iota(jnp.int32, (8, 128), 0)
    for s in range(8):
        band = jnp.broadcast_to(bands_ref[s : s + 1, :], (8, 128))
        total = (band == kinds8).astype(F32)
        for i in range(NB):
            picked = jnp.zeros((8, 128), F32)
            column = jnp.zeros((8, 128), F32)
            for k in range(NB):
                picked = jnp.where(band == k, mix_ref[k, i], picked)
                column = jnp.where(kinds8 == k, mix_ref[k, i], column)
            total = total + column * picked
        high = total.astype(BF16).astype(F32)
        rest = total - high
        middle = rest.astype(BF16).astype(F32)
        low = rest - middle
        zeros = jnp.zeros((104, 128), F32)
        tab[:, s * 128 : (s + 1) * 128] = jnp.concatenate([high, middle, low, zeros], axis=0).astype(BF16)
    mpad[...] = jnp.concatenate([m_in[...].astype(F32), jnp.zeros((8, MB), F32)], axis=0).astype(BF16)

    plan_col = jnp.sum(jnp.where(lan == me, plan, 0), axis=1, keepdims=True)
    before = jnp.sum(jnp.where(sub < lan, plan_col, 0), axis=0, keepdims=True)
    sub16 = lax.broadcasted_iota(jnp.int32, (16, 32), 0)
    lan16 = lax.broadcasted_iota(jnp.int32, (16, 32), 1)
    source = jnp.sum((before <= sub16).astype(jnp.int32), axis=1, keepdims=True) - 1
    source_hot = (lan16 == source).astype(F32)

    gw.step(0, 1)
    gw.step(1, 0)
    gl.begin()

    def route_all():
        others = pl.ds(0, 31)
        return remote(sendbuf.at[others], incoming.at[others], route_s, route_r, ((me + 1) % 32, ib))

    route_all().wait_recv()

    st = ROOT / jnp.full((1, 128), ls_ref[0], F32)
    sw = ROOT / jnp.full((1, 128), ls_ref[1], F32)
    code = exact_pick(source_hot, incoming[:, 2, :])
    label = jnp.zeros((16, 128), F32)
    for n in range(1, C):
        label = label + (code >= float(NB * n)).astype(F32)
    band = code - float(NB) * label
    feat[:, 0, :] = exact_pick(source_hot, incoming[:, 0, :]) * st
    feat[:, 1, :] = exact_pick(source_hot, incoming[:, 1, :]) * sw
    feat[:, 2, :] = band
    for k in range(3, 8):
        feat[:, k, :] = jnp.zeros((16, 128), F32)
    for k in range(16):
        lanes = slice((k % 2) * 128, (k % 2) * 128 + 128)
        crow[k // 2, 0:1, lanes] = label[k : k + 1, :]
        crow[k // 2, 1:2, lanes] = band[k : k + 1, :]

    lane = lax.broadcasted_iota(jnp.int32, (128, 128), 1)
    kind = (lane % 8).astype(F32)
    live = lane < 24

    def cov_block(b, carry):
        cols = jnp.transpose(feat[b])
        t = cols[:, 0:1]
        w = cols[:, 1:2]
        hot = jnp.where(live & (cols[:, 2:3] == kind), 1.0, 0.0).astype(BF16)
        rows = pl.ds(pl.multiple_of(b * 128, 128), 128)
        for s in range(4):
            lanes = slice(s * 256, s * 256 + 256)
            dt = t - centers_s[0:1, lanes]
            dw = w - centers_s[1:2, lanes]
            mixing = dot_nn(hot, tab[:, lanes])
            kbuf[rows, lanes] = (jnp.exp2(-(dt * dt + dw * dw)) * mixing).astype(BF16)
        return carry

    order = (
        (2, ((gw, 0, 2),)),
        (4, ((gw, 1, 1),)),
        (6, ((gl, 0, 1), (gl, 1, 0))),
        (8, ((gw, 0, 3),)),
        (10, ((gw, 1, 2), (gl, 0, 2))),
        (13, ((gw, 0, 4), (gl, 1, 1))),
        (16, ((gl, 0, 3), (gw, 1, 3), (gl, 1, 2), (gw, 1, 4))),
    )
    done = 0
    for upto, events in order:
        lax.fori_loop(done, upto, cov_block, 0)
        done = upto
        for g, stream, k in events:
            g.step(stream, k)
    gw.end()

    turn = 0
    plan_l = {3: (0, 4), 9: (1, 3), 13: (1, 4)}
    for part in range(4):
        rows = slice(part * 512, part * 512 + 512)
        for n in range(4):
            lanes = slice(n * 256, n * 256 + 256)
            a = dot_nn(kbuf[rows, :], wbuf[:, :, :, :, lanes].reshape(MB, 256))
            abuf[rows, lanes] = a.astype(BF16)
            squares = a[:, :128] * a[:, :128] + a[:, 128:] * a[:, 128:]
            if n == 0:
                sq[rows, :] = squares
            else:
                sq[rows, :] += squares
            if turn in plan_l:
                gl.step(*plan_l[turn])
            turn += 1
    def flip(i, carry):
        rows = pl.ds(pl.multiple_of(i * 256, 256), 256)
        atbuf[:, rows] = jnp.transpose(abuf[rows, :])
        return carry

    lax.fori_loop(0, 4, flip, 0)
    gl.end()

    class_ids = lax.broadcasted_iota(jnp.int32, (8, 256), 0)
    scale = jnp.zeros((8, 256), F32)
    for n in range(C):
        scale = jnp.where(class_ids == n, scales_ref[n], scale)

    chunks = ((0, 2), (2, 2), (4, 2), (6, 1), (7, 1))

    def term_slot(src, i):
        first, many = chunks[i]
        return terms.at[src, pl.ds(first, many)]

    def term_copy(i, d):
        slot = term_slot(ib, i)
        return remote(slot, slot, st_s, st_r.at[i], (me, (ib + d) % 8))

    def b_chunk(i):
        first, many = chunks[i]
        lo, size = first * 256, many * 256
        rows = slice(lo, lo + size)
        squares = -sq[rows, :]
        for n in range(4):
            lanes = slice(n * 256, n * 256 + 256)
            deep = slice(n * 256, MB)
            lower = lbuf[2 * n :, :, :, :, lanes].reshape(MB - n * 256, 256)
            b = dot_nn(abuf[rows, deep], lower)
            bbuf[rows, lanes] = b
            squares = squares + (b[:, :128] * b[:, :128] + b[:, 128:] * b[:, 128:])
        means = dot_nt(mpad[...], abuf[rows, :])[0:8, :]
        var = jnp.sum(jnp.transpose(squares), axis=0, keepdims=True)
        for k in range(many):
            lanes = slice(k * 256, k * 256 + 256)
            terms[ib, first + k] = means[:, lanes] + 0.5 * scale * var[:, lanes]

        def send(d, carry):
            term_copy(i, d).start()
            return carry

        lax.fori_loop(1, 8, send, 0)

    for i in range(5):
        b_chunk(i)

    def term_wait(i):
        first, many = chunks[i]
        slot = terms.at[pl.ds(0, 7), pl.ds(first, many)]
        remote(slot, slot, st_s, st_r.at[i], (me, (ib + 1) % 8)).wait_recv()

    values = []
    for k in range(NB):
        value = jnp.float32(1.0)
        for i in range(NB):
            value = value + mix_ref[k, i] * mix_ref[k, i]
        values.append(value)
    classes = class_ids.astype(F32)

    def likelihood(p):
        lanes = slice(p * 256, p * 256 + 256)
        logits = terms[0, p]
        for q in range(1, 8):
            logits = logits + terms[q, p]
        band = crow[p, 1:2, :]
        own = jnp.zeros((1, 256), F32)
        for k in range(NB):
            own = jnp.where(band == float(k), values[k], own)
        weights = jnp.exp(logits + 0.5 * scale * own)
        ch = weights / jnp.sum(weights, axis=0, keepdims=True)
        probs_out[:, lanes] = ch
        slope = jnp.where(crow[p, 0:1, :] == classes, 1.0, 0.0) - ch
        ms[:, lanes] = jnp.concatenate([slope, jnp.zeros((8, 256), F32)], axis=0).astype(BF16)
        slope = -jnp.sum(ch * scale, axis=0, keepdims=True)
        column = jnp.transpose(jnp.broadcast_to(slope, (8, 256)))[:, 0:1]
        rows = slice(p * 256, p * 256 + 256)
        hbuf[rows, :] = (column * bbuf[rows, :]).astype(BF16)

    lax.fori_loop(4, 8, flip, 0)
    term_wait(0)
    term_wait(1)
    for p in range(4):
        likelihood(p)
    mt0[...] = dot_nn(ms[:, 0:1024], abuf[0:1024, :])[0:8, :]
    for n in range(4):
        lanes = slice(n * 256, n * 256 + 256)
        for lo in range(n * 256, MB, 512):
            hi = min(lo + 512, MB)
            bbuf[lo:hi, lanes] = dot_nn(atbuf[lo:hi, 0:1024], hbuf[0:1024, lanes])
    for i in range(2, 5):
        term_wait(i)
    for p in range(4, 8):
        likelihood(p)

    mt0[...] += dot_nn(ms[:, 1024:2048], abuf[1024:2048, :])[0:8, :]
    mean1 = remote(mt0, rm1, m12_s.at[0], m12_r.at[0], at(z, xh, oc))
    mean1.start()

    colour = xh * 2 + c

    def m3_copy(d):
        return remote(mt2.at[colour], rm3.at[z], m3_s, m3_r, at((z + d) % 8, xh, c))

    def m4_copy(k):
        dev = (at(z, xh, oc), at(z, oxh, c), at(z, oxh, oc))[k]
        return remote(quarters.at[colour], quarters.at[colour], m4_s, m4_r, dev)

    mean2 = remote(mt1, rm2, m12_s.at[1], m12_r.at[1], at(z, oxh, c))

    def p1_copy(n):
        lanes = pl.ds(n * 256, 256)
        return remote(
            gbuf.at[pl.ds(2 * n, 8 - 2 * n), :, oc, :, lanes],
            r1.at[pl.ds(2 * n, 8 - 2 * n), :, :, lanes],
            p1_s.at[n], p1_r.at[n], at(z, xh, oc),
        )

    def p2_copy(n):
        lanes = pl.ds(n * 256, 256)
        return remote(
            s1.at[pl.ds(2 * n, 8 - 2 * n), oxh, :, lanes],
            r2.at[pl.ds(2 * n, 8 - 2 * n), :, lanes],
            p2_s.at[n], p2_r.at[n], at(z, oxh, c),
        )

    def p3_copy(n, zz):
        lanes = pl.ds(n * 256, 256)
        return remote(
            s2.at[zz, :, lanes], r3.at[z, :, lanes], p3_s.at[n], p3_r.at[n], at(zz, xh, c)
        )

    def stage1(n):
        lanes = slice(n * 256, n * 256 + 256)
        for lo in range(n * 256, MB, 512):
            hi = min(lo + 512, MB)
            g = dot_nn(atbuf[lo:hi, 1024:2048], hbuf[1024:2048, lanes])
            g = (g + bbuf[lo:hi, lanes]).astype(BF16)
            gbuf[lo // 128 : hi // 128, :, :, :, lanes] = g.reshape((hi - lo) // 128, 2, 2, 32, 256)
        p1_copy(n).start()

    def stage2(n):
        p1_copy(n).wait_recv()
        lanes = pl.ds(n * 256, 256)

        def add(zz, carry):
            for j in range(2):
                total = gbuf[zz, j, c, :, lanes].astype(F32) + r1[zz, j, :, lanes].astype(F32)
                s1[zz, j, :, lanes] = total.astype(BF16)
            return carry

        lax.fori_loop(2 * n, 8, add, 0)
        p2_copy(n).start()

    def stage3(n):
        p2_copy(n).wait_recv()
        lanes = pl.ds(n * 256, 256)

        def add(zz, carry):
            total = s1[zz, xh, :, lanes].astype(F32) + r2[zz, :, lanes].astype(F32)
            s2[zz, :, lanes] = total.astype(BF16)

            @pl.when(zz != z)
            def _():
                p3_copy(n, zz).start()

            @pl.when(zz == z)
            def _():
                r3[z, :, lanes] = total.astype(BF16)

            return carry

        lax.fori_loop(2 * n, 8, add, 0)

    def m3_start(d, carry):
        m3_copy(d).start()
        return carry

    def m3_all():
        return remote(rm3.at[pl.ds(0, 7)], rm3.at[pl.ds(0, 7)], m3_s, m3_r, at(zp, xh, c))

    def m4_all():
        return remote(quarters.at[pl.ds(0, 3)], quarters.at[pl.ds(0, 3)], m4_s, m4_r, at(z, xh, oc))

    stage1(0)
    mean1.wait_recv()
    mt1[...] = mt0[...] + rm1[...]
    mean2.start()
    stage1(1)
    stage2(0)
    stage1(2)
    stage2(1)
    stage1(3)
    stage2(2)
    stage2(3)
    mean2.wait_recv()
    for k in range(4):
        lanes = slice(k * 256, k * 256 + 256)
        mt2[k] = mt1[:, lanes] + rm2[:, lanes]
    rm3[z] = mt2[colour]
    lax.fori_loop(1, 8, m3_start, 0)
    stage3(0)
    stage3(1)
    m3_all().wait_recv()
    grad = rm3[0]
    for p in range(1, 8):
        grad = grad + rm3[p]
    quarters[colour] = grad
    for k in range(3):
        m4_copy(k).start()
    stage3(2)
    stage3(3)
    m4_all().wait_recv()
    for k in range(4):
        lanes = slice(k * 256, k * 256 + 256)
        gmean_out[:, lanes] = quarters[k] - m_in[:, lanes].astype(F32)

    def p3_all(n, many):
        lanes = pl.ds(n * 256, 256)
        return remote(
            s2.at[pl.ds(0, many), :, lanes], r3.at[pl.ds(0, many), :, lanes], p3_s.at[n], p3_r.at[n], at(zp, xh, c)
        )

    def p3_wait(n):
        @pl.when(z >= 2 * n)
        def _():
            p3_all(n, 7).wait_recv()

    for n in range(4):
        p3_wait(n)
    data = r3[0].astype(F32)
    for p in range(1, 8):
        data = data + r3[p].astype(F32)
    column_ids = lax.broadcasted_iota(jnp.int32, (32, MB), 1)
    row_ids = lax.broadcasted_iota(jnp.int32, (32, MB), 0) + me * 32
    own_chol = lbuf[z, xh, c].astype(F32)
    on_diag = column_ids == row_ids
    diagonal = jnp.sum(jnp.where(on_diag, own_chol, 0.0), axis=1, keepdims=True)
    gchol_out[...] = (
        jnp.where(column_ids <= row_ids, data, 0.0) - own_chol + jnp.where(on_diag, 1.0 / diagonal, 0.0)
    )

    route_all().wait_send()
    gw.drain()
    gl.drain()

    slot = terms.at[pl.ds(0, 7)]
    remote(slot, slot, st_s, st_r.at[0], (me, (ib + 1) % 8)).wait_send()
    mean1.wait_send()
    mean2.wait_send()
    m3_all().wait_send()
    m4_all().wait_send()
    for n in range(4):
        p1_copy(n).wait_send()
        p2_copy(n).wait_send()

        @pl.when(z >= 2 * n)
        def _():
            p3_all(n, 7 - 2 * n).wait_send()

        @pl.when(z < 2 * n)
        def _():
            p3_all(n, 8 - 2 * n).wait_send()


def body(
    obs_coords, obs_codes, route_plan, inducing_coords, inducing_bands, band_mix, lengthscales,
    class_scales, prior_factor, variational_chol, variational_mean,
):
    vmem = pl.BlockSpec(memory_space=pltpu.VMEM)
    whole = pl.BlockSpec(memory_space=pl.ANY)
    smem = pl.BlockSpec(memory_space=pltpu.SMEM)
    dma = pltpu.SemaphoreType.DMA
    return pl.pallas_call(
        kernel,
        out_shape=(
            pltpu.VMEM((C, ROWS), F32),
            pltpu.VMEM((32, MB), F32),
            pltpu.VMEM((C, MB), F32),
        ),
        in_specs=[whole] * 5 + [smem] * 3 + [whole] * 3,
        out_specs=(vmem, vmem, vmem),
        scratch_shapes=[
            pltpu.VMEM((2, 4096), F32),
            pltpu.VMEM((32, 128), jnp.int32),
            pltpu.VMEM((32, 32), jnp.int32),
            pltpu.VMEM((2, MB), F32),
            pltpu.VMEM((8, 128), jnp.int32),
            pltpu.VMEM((C, MB), BF16),
            dma((8,)),
            pltpu.VMEM((2, 32, 128), F32),
            pltpu.VMEM((32, 4, 128), F32),
            pltpu.VMEM((32, 4, 128), F32),
            pltpu.VMEM((16, 8, 128), F32),
            pltpu.VMEM((8, 2, 256), F32),
            pltpu.VMEM((128, MB), BF16),
            pltpu.VMEM((2, MB), F32),
            pltpu.VMEM((16, MB), BF16),
            pltpu.VMEM((8, 2, 2, 32, MB), BF16),
            pltpu.VMEM((8, 2, 2, 32, MB), BF16),
            pltpu.VMEM((ROWS, MB), BF16),
            pltpu.VMEM((ROWS, MB), BF16),
            pltpu.VMEM((MB, ROWS), BF16),
            pltpu.VMEM((ROWS, MB), F32),
            pltpu.VMEM((ROWS, MB), BF16),
            pltpu.VMEM((ROWS, 128), F32),
            pltpu.VMEM((8, 8, 8, 256), F32),
            pltpu.VMEM((16, ROWS), BF16),
            pltpu.VMEM((8, 2, 2, 32, MB), BF16),
            pltpu.VMEM((8, 2, 32, MB), BF16),
            pltpu.VMEM((8, 2, 32, MB), BF16),
            pltpu.VMEM((8, 32, MB), BF16),
            pltpu.VMEM((8, 32, MB), BF16),
            pltpu.VMEM((8, 32, MB), BF16),
            pltpu.VMEM((8, MB), F32),
            pltpu.VMEM((8, MB), F32),
            pltpu.VMEM((4, 8, 256), F32),
            pltpu.VMEM((8, MB), F32),
            pltpu.VMEM((8, MB), F32),
            pltpu.VMEM((8, 8, 256), F32),
            pltpu.VMEM((4, 8, 256), F32),
            dma(()), dma(()), dma((8,)), dma((16,)), dma((8,)), dma((16,)),
            dma(()), dma((5,)),
            dma((4,)), dma((4,)), dma((4,)), dma((4,)), dma((4,)), dma((4,)),
            dma((2,)), dma((2,)), dma(()), dma(()), dma(()), dma(()),
        ],
        compiler_params=pltpu.CompilerParams(
            collective_id=0, has_side_effects=True, vmem_limit_bytes=60 << 20
        ),
        name="elbo_step",
    )(
        obs_coords, obs_codes.reshape(32, 128), route_plan, inducing_coords,
        inducing_bands.reshape(8, 128), band_mix, lengthscales, class_scales,
        prior_factor, variational_chol, variational_mean,
    )


def solution(mesh):
    placed = (
        P(None, "obs"), P("obs"), P(), P(None, "ind"), P("ind"), P(), P(), P(),
        P(("ind", "obs"), None), P(("ind", "obs"), None), P(None, "ind"),
    )
    return jax.shard_map(
        body,
        mesh=mesh,
        in_specs=placed,
        out_specs=(P(None, "obs"), P(("ind", "obs"), None), P(None, "ind")),
        check_vma=False,
    )
```

```python
import functools
import math

import jax
import jax.numpy as jnp
from jax import lax
from jax.experimental import pallas as pl
from jax.experimental.pallas import tpu as pltpu
from jax.sharding import PartitionSpec as P

C = 8
NB = 6
ROWS = 2048
MB = 1024
MESH = pl.DeviceIdType.MESH
F32 = jnp.float32
BF16 = jnp.bfloat16
ROOT = math.sqrt(0.5 * math.log2(math.e))


def dot_nn(a, b):
    return jnp.dot(a, b, preferred_element_type=F32)


def dot_nt(a, b):
    return lax.dot_general(a, b, (((1,), (1,)), ((), ())), preferred_element_type=F32)


def exact_pick(hot, rows):
    return jnp.dot(hot, rows, precision=lax.Precision.HIGHEST, preferred_element_type=F32)


def kernel(
    coords_in, codes_in, plan_in, centers_in, bands_in, mix_ref, ls_ref, scales_ref,
    w_in, l_in, m_any,
    probs_out, gchol_out, gmean_out,
    coords_ref, codes_ref, plan_ref, centers_ref, bands_ref, m_in, load_sem,
    held, sendbuf, incoming, feat, crow, tab, centers_s, mpad,
    wbuf, lbuf, kbuf, abuf, atbuf, bbuf, hbuf, sq,
    terms, ms,
    gbuf, r1, s1, r2, s2, r3,
    mt0, mt1, mt2, rm1, rm2, rm3, quarters,
    route_s, route_r, agw_s, agw_r, agl_s, agl_r,
    st_s, st_r, p1_s, p1_r, p2_s, p2_r, p3_s, p3_r,
    m12_s, m12_r, m3_s, m3_r, m4_s, m4_r,
):
    me = lax.axis_index("obs")
    ib = lax.axis_index("ind")
    z = me // 4
    xh = (me // 2) % 2
    c = me % 2
    oxh = 1 - xh
    oc = 1 - c
    zp = (z + 1) % 8
    zm = (z + 7) % 8

    def at(zz, xx, cc):
        return (zz * 4 + xx * 2 + cc, ib)

    def remote(src, dst, ssem, rsem, dev):
        return pltpu.make_async_remote_copy(
            src_ref=src, dst_ref=dst, send_sem=ssem, recv_sem=rsem, device_id=dev, device_id_type=MESH
        )

    loads = [
        pltpu.make_async_copy(src, dst, load_sem.at[k])
        for k, (src, dst) in enumerate((
            (coords_in, coords_ref), (codes_in, codes_ref), (plan_in, plan_ref),
            (w_in, wbuf.at[z, xh, c]), (l_in, lbuf.at[z, xh, c]),
            (centers_in, centers_ref), (bands_in, bands_ref), (m_any, m_in),
        ))
    ]
    for copy in loads:
        copy.start()
    r3[...] = jnp.zeros_like(r3)

    barrier = pltpu.get_barrier_semaphore()

    def greet_obs(d, carry):
        pl.semaphore_signal(barrier, inc=1, device_id=((me + d) % 32, ib), device_id_type=MESH)
        return carry

    def greet_ind(d, carry):
        pl.semaphore_signal(barrier, inc=1, device_id=(me, (ib + d) % 8), device_id_type=MESH)
        return carry

    lax.fori_loop(1, 32, greet_obs, 0)
    lax.fori_loop(1, 8, greet_ind, 0)

    for copy in loads:
        copy.wait()
    for b in range(32):
        held[0, b : b + 1, :] = coords_ref[0:1, b * 128 : b * 128 + 128]
        held[1, b : b + 1, :] = coords_ref[1:2, b * 128 : b * 128 + 128]
    plan = plan_ref[...]
    sub = lax.broadcasted_iota(jnp.int32, (32, 32), 0)
    lan = lax.broadcasted_iota(jnp.int32, (32, 32), 1)
    plan_row = jnp.sum(jnp.where(sub == me, plan, 0), axis=0, keepdims=True)
    start = jnp.sum(jnp.where(lan < sub, plan_row, 0), axis=1, keepdims=True)
    choose = (lan == start).astype(F32)
    sendbuf[:, 0, :] = exact_pick(choose, held[0])
    sendbuf[:, 1, :] = exact_pick(choose, held[1])
    sendbuf[:, 2, :] = exact_pick(choose, codes_ref[...].astype(F32))
    sendbuf[:, 3, :] = jnp.zeros((32, 128), F32)
    incoming[me] = sendbuf[me]

    pl.semaphore_wait(barrier, 38)

    def route_copy(d):
        peer = (me + d) % 32
        return remote(sendbuf.at[peer], incoming.at[me], route_s, route_r, (peer, ib))

    def route_start(d, carry):
        route_copy(d).start()
        return carry

    class Gather:
        def __init__(self, buf, ss, rs, triangular):
            self.buf, self.ss, self.rs, self.triangular = buf, ss, rs, triangular

        def widths(self, zz, fn):
            if not self.triangular:
                fn(slice(None))
                return
            for v in range(4):

                @pl.when(zz // 2 == v)
                def _():
                    fn(pl.ds(0, (v + 1) * 256))

        def go(self, op, q, j, cc, idx, dev):
            zz = self.unit(q)

            def fn(lanes):
                slot = self.buf.at[zz, j, cc, :, lanes] if self.triangular else self.buf.at[zz, j, cc]
                getattr(remote(slot, slot, self.ss.at[q], self.rs.at[idx], dev), op)()

            self.widths(zz, fn)

        def unit(self, q):
            return (z + (0, 7, 6, 5, 1, 2, 3, 4)[q]) % 8

        def half(self, stream):
            return xh if stream == 0 else oxh

        def along(self, op, stream, q, hops, to):
            idx = 7 * stream + to
            self.go(op, q, self.half(stream), c, idx, at((z + 8 + hops) % 8, xh, c))

        def fourth(self, op):
            for j in range(2):

                @pl.when(xh == j)
                def _():
                    self.along(op, 0, 3 + 3 * j, 1 - 2 * j, 7)

        def core(self, op, stream, q):
            self.go(op, q, self.half(stream), c, 15, at(z, xh, oc))

        def across(self, op, q):
            self.go(op, q, xh, c, 7 + q if q else 0, at(z, oxh, c))

        def wait(self, stream, q):
            idx = 7 * stream + q if q else 0
            self.go("wait_recv", q, self.half(stream), c, idx, at(z, oxh, c))

        def begin(self):
            self.along("start", 0, 0, 1, 1)
            self.along("start", 0, 0, -1, 4)
            self.across("start", 0)
            self.core("start", 0, 0)

        def step(self, stream, k):
            if k == 0:
                self.wait(1, 0)
                self.along("start", 1, 0, 1, 1)
                self.along("start", 1, 0, -1, 4)
                self.core("start", 1, 0)
                return
            if k == 4:
                self.wait(stream, 7)
                if stream == 0:
                    self.across("start", 7)
                self.core("start", stream, 7)
                return
            relay = k < 3 - stream
            self.wait(stream, k)
            if relay:
                self.along("start", stream, k, 1, k + 1)
            self.wait(stream, 3 + k)
            if relay:
                self.along("start", stream, 3 + k, -1, 4 + k)
            if stream == 0 and k == 3:
                self.fourth("start")
                self.across("start", 3)
                self.across("start", 6)
            self.core("start", stream, k)
            self.core("start", stream, 3 + k)

        def end(self):
            rows = pl.ds(0, 320 if self.triangular else 512)
            remote(kbuf.at[rows], abuf.at[rows], self.ss.at[0], self.rs.at[15], at(z, xh, oc)).wait_recv()

        def drain(self):
            for q in range(8):
                many = (7, 4, 3, 3, 4, 3, 3, 3)[q]

                def settle(count):
                    def fn(lanes):
                        rows = pl.ds(0, 32 * count)
                        remote(
                            kbuf.at[rows, lanes], abuf.at[rows, lanes], self.ss.at[q], self.rs.at[15], at(z, xh, oc)
                        ).wait_send()

                    self.widths(self.unit(q), fn)

                if q in (3, 6):
                    pl.when(xh == (q - 3) // 3)(functools.partial(settle, many + 1))
                    pl.when(xh != (q - 3) // 3)(functools.partial(settle, many))
                else:
                    settle(many)

    gw = Gather(wbuf, agw_s, agw_r, False)
    gl = Gather(lbuf, agl_s, agl_r, True)
    gw.begin()
    lax.fori_loop(1, 32, route_start, 0)

    ls0 = jnp.full((1, MB), ls_ref[0], F32)
    ls1 = jnp.full((1, MB), ls_ref[1], F32)
    centers_s[0:1, :] = centers_ref[0:1, :] * (ROOT / ls0)
    centers_s[1:2, :] = centers_ref[1:2, :] * (ROOT / ls1)
    kinds8 = lax.broadcasted_iota(jnp.int32, (8, 128), 0)
    for s in range(8):
        band = jnp.broadcast_to(bands_ref[s : s + 1, :], (8, 128))
        total = (band == kinds8).astype(F32)
        for i in range(NB):
            picked = jnp.zeros((8, 128), F32)
            column = jnp.zeros((8, 128), F32)
            for k in range(NB):
                picked = jnp.where(band == k, mix_ref[k, i], picked)
                column = jnp.where(kinds8 == k, mix_ref[k, i], column)
            total = total + column * picked
        high = total.astype(BF16).astype(F32)
        rest = total - high
        middle = rest.astype(BF16).astype(F32)
        low = rest - middle
        zeros = jnp.zeros((104, 128), F32)
        tab[:, s * 128 : (s + 1) * 128] = jnp.concatenate([high, middle, low, zeros], axis=0).astype(BF16)
    mpad[...] = jnp.concatenate([m_in[...].astype(F32), jnp.zeros((8, MB), F32)], axis=0).astype(BF16)

    plan_col = jnp.sum(jnp.where(lan == me, plan, 0), axis=1, keepdims=True)
    before = jnp.sum(jnp.where(sub < lan, plan_col, 0), axis=0, keepdims=True)
    sub16 = lax.broadcasted_iota(jnp.int32, (16, 32), 0)
    lan16 = lax.broadcasted_iota(jnp.int32, (16, 32), 1)
    source = jnp.sum((before <= sub16).astype(jnp.int32), axis=1, keepdims=True) - 1
    source_hot = (lan16 == source).astype(F32)

    gw.step(0, 1)
    gw.step(1, 0)
    gl.begin()

    def route_all():
        others = pl.ds(0, 31)
        return remote(sendbuf.at[others], incoming.at[others], route_s, route_r, ((me + 1) % 32, ib))

    route_all().wait_recv()

    st = ROOT / jnp.full((1, 128), ls_ref[0], F32)
    sw = ROOT / jnp.full((1, 128), ls_ref[1], F32)
    code = exact_pick(source_hot, incoming[:, 2, :])
    label = jnp.zeros((16, 128), F32)
    for n in range(1, C):
        label = label + (code >= float(NB * n)).astype(F32)
    band = code - float(NB) * label
    feat[:, 0, :] = exact_pick(source_hot, incoming[:, 0, :]) * st
    feat[:, 1, :] = exact_pick(source_hot, incoming[:, 1, :]) * sw
    feat[:, 2, :] = band
    for k in range(3, 8):
        feat[:, k, :] = jnp.zeros((16, 128), F32)
    for k in range(16):
        lanes = slice((k % 2) * 128, (k % 2) * 128 + 128)
        crow[k // 2, 0:1, lanes] = label[k : k + 1, :]
        crow[k // 2, 1:2, lanes] = band[k : k + 1, :]

    lane = lax.broadcasted_iota(jnp.int32, (128, 128), 1)
    kind = (lane % 8).astype(F32)
    live = lane < 24

    def cov_block(b, carry):
        cols = jnp.transpose(feat[b])
        t = cols[:, 0:1]
        w = cols[:, 1:2]
        hot = jnp.where(live & (cols[:, 2:3] == kind), 1.0, 0.0).astype(BF16)
        rows = pl.ds(pl.multiple_of(b * 128, 128), 128)
        for s in range(4):
            lanes = slice(s * 256, s * 256 + 256)
            dt = t - centers_s[0:1, lanes]
            dw = w - centers_s[1:2, lanes]
            mixing = dot_nn(hot, tab[:, lanes])
            kbuf[rows, lanes] = (jnp.exp2(-(dt * dt + dw * dw)) * mixing).astype(BF16)
        return carry

    order = (
        (2, ((gw, 0, 2),)),
        (4, ((gw, 1, 1),)),
        (6, ((gl, 0, 1), (gl, 1, 0))),
        (8, ((gw, 0, 3),)),
        (10, ((gw, 1, 2), (gl, 0, 2))),
        (13, ((gw, 0, 4), (gl, 1, 1))),
        (16, ((gw, 1, 3), (gl, 0, 3), (gw, 1, 4), (gl, 1, 2))),
    )
    done = 0
    for upto, events in order:
        lax.fori_loop(done, upto, cov_block, 0)
        done = upto
        for g, stream, k in events:
            g.step(stream, k)
    gw.end()

    turn = 0
    plan_l = {3: (0, 4), 9: (1, 3), 13: (1, 4)}
    for part in range(4):
        rows = slice(part * 512, part * 512 + 512)
        for n in range(4):
            lanes = slice(n * 256, n * 256 + 256)
            a = dot_nn(kbuf[rows, :], wbuf[:, :, :, :, lanes].reshape(MB, 256))
            abuf[rows, lanes] = a.astype(BF16)
            squares = a[:, :128] * a[:, :128] + a[:, 128:] * a[:, 128:]
            if n == 0:
                sq[rows, :] = squares
            else:
                sq[rows, :] += squares
            if turn in plan_l:
                gl.step(*plan_l[turn])
            turn += 1
    def flip(i, carry):
        rows = pl.ds(pl.multiple_of(i * 256, 256), 256)
        atbuf[:, rows] = jnp.transpose(abuf[rows, :])
        return carry

    lax.fori_loop(0, 4, flip, 0)
    gl.end()

    class_ids = lax.broadcasted_iota(jnp.int32, (8, 256), 0)
    scale = jnp.zeros((8, 256), F32)
    for n in range(C):
        scale = jnp.where(class_ids == n, scales_ref[n], scale)

    chunks = ((0, 2), (2, 2), (4, 2), (6, 1), (7, 1))

    def term_slot(src, i):
        first, many = chunks[i]
        return terms.at[src, pl.ds(first, many)]

    def term_copy(i, d):
        slot = term_slot(ib, i)
        return remote(slot, slot, st_s, st_r.at[i], (me, (ib + d) % 8))

    def b_chunk(i):
        first, many = chunks[i]
        lo, size = first * 256, many * 256
        rows = slice(lo, lo + size)
        squares = -sq[rows, :]
        for n in range(4):
            lanes = slice(n * 256, n * 256 + 256)
            deep = slice(n * 256, MB)
            lower = lbuf[2 * n :, :, :, :, lanes].reshape(MB - n * 256, 256)
            b = dot_nn(abuf[rows, deep], lower)
            bbuf[rows, lanes] = b
            squares = squares + (b[:, :128] * b[:, :128] + b[:, 128:] * b[:, 128:])
        means = dot_nt(mpad[...], abuf[rows, :])[0:8, :]
        var = jnp.sum(jnp.transpose(squares), axis=0, keepdims=True)
        for k in range(many):
            lanes = slice(k * 256, k * 256 + 256)
            terms[ib, first + k] = means[:, lanes] + 0.5 * scale * var[:, lanes]

        def send(d, carry):
            term_copy(i, d).start()
            return carry

        lax.fori_loop(1, 8, send, 0)

    for i in range(5):
        b_chunk(i)

    def term_wait(i):
        first, many = chunks[i]
        slot = terms.at[pl.ds(0, 7), pl.ds(first, many)]
        remote(slot, slot, st_s, st_r.at[i], (me, (ib + 1) % 8)).wait_recv()

    values = []
    for k in range(NB):
        value = jnp.float32(1.0)
        for i in range(NB):
            value = value + mix_ref[k, i] * mix_ref[k, i]
        values.append(value)
    classes = class_ids.astype(F32)

    def likelihood(p):
        lanes = slice(p * 256, p * 256 + 256)
        logits = terms[0, p]
        for q in range(1, 8):
            logits = logits + terms[q, p]
        band = crow[p, 1:2, :]
        own = jnp.zeros((1, 256), F32)
        for k in range(NB):
            own = jnp.where(band == float(k), values[k], own)
        weights = jnp.exp(logits + 0.5 * scale * own)
        ch = weights / jnp.sum(weights, axis=0, keepdims=True)
        probs_out[:, lanes] = ch
        slope = jnp.where(crow[p, 0:1, :] == classes, 1.0, 0.0) - ch
        ms[:, lanes] = jnp.concatenate([slope, jnp.zeros((8, 256), F32)], axis=0).astype(BF16)
        slope = -jnp.sum(ch * scale, axis=0, keepdims=True)
        column = jnp.transpose(jnp.broadcast_to(slope, (8, 256)))[:, 0:1]
        rows = slice(p * 256, p * 256 + 256)
        hbuf[rows, :] = (column * bbuf[rows, :]).astype(BF16)

    lax.fori_loop(4, 8, flip, 0)
    term_wait(0)
    term_wait(1)
    for p in range(4):
        likelihood(p)
    mt0[...] = dot_nn(ms[:, 0:1024], abuf[0:1024, :])[0:8, :]
    for n in range(4):
        lanes = slice(n * 256, n * 256 + 256)
        for lo in range(n * 256, MB, 512):
            hi = min(lo + 512, MB)
            bbuf[lo:hi, lanes] = dot_nn(atbuf[lo:hi, 0:1024], hbuf[0:1024, lanes])
    for i in range(2, 5):
        term_wait(i)
    for p in range(4, 8):
        likelihood(p)

    mt0[...] += dot_nn(ms[:, 1024:2048], abuf[1024:2048, :])[0:8, :]
    mean1 = remote(mt0, rm1, m12_s.at[0], m12_r.at[0], at(z, xh, oc))
    mean1.start()

    colour = xh * 2 + c

    def m3_copy(d):
        return remote(mt2.at[colour], rm3.at[z], m3_s, m3_r, at((z + d) % 8, xh, c))

    def m4_copy(k):
        dev = (at(z, xh, oc), at(z, oxh, c), at(z, oxh, oc))[k]
        return remote(quarters.at[colour], quarters.at[colour], m4_s, m4_r, dev)

    mean2 = remote(mt1, rm2, m12_s.at[1], m12_r.at[1], at(z, oxh, c))

    def p1_copy(n):
        lanes = pl.ds(n * 256, 256)
        return remote(
            gbuf.at[pl.ds(2 * n, 8 - 2 * n), :, oc, :, lanes],
            r1.at[pl.ds(2 * n, 8 - 2 * n), :, :, lanes],
            p1_s.at[n], p1_r.at[n], at(z, xh, oc),
        )

    def p2_copy(n):
        lanes = pl.ds(n * 256, 256)
        return remote(
            s1.at[pl.ds(2 * n, 8 - 2 * n), oxh, :, lanes],
            r2.at[pl.ds(2 * n, 8 - 2 * n), :, lanes],
            p2_s.at[n], p2_r.at[n], at(z, oxh, c),
        )

    def p3_copy(n, zz):
        lanes = pl.ds(n * 256, 256)
        return remote(
            s2.at[zz, :, lanes], r3.at[z, :, lanes], p3_s.at[n], p3_r.at[n], at(zz, xh, c)
        )

    def stage1(n):
        lanes = slice(n * 256, n * 256 + 256)
        for lo in range(n * 256, MB, 512):
            hi = min(lo + 512, MB)
            g = dot_nn(atbuf[lo:hi, 1024:2048], hbuf[1024:2048, lanes])
            g = (g + bbuf[lo:hi, lanes]).astype(BF16)
            gbuf[lo // 128 : hi // 128, :, :, :, lanes] = g.reshape((hi - lo) // 128, 2, 2, 32, 256)
        p1_copy(n).start()

    def stage2(n):
        p1_copy(n).wait_recv()
        lanes = pl.ds(n * 256, 256)

        def add(zz, carry):
            for j in range(2):
                total = gbuf[zz, j, c, :, lanes].astype(F32) + r1[zz, j, :, lanes].astype(F32)
                s1[zz, j, :, lanes] = total.astype(BF16)
            return carry

        lax.fori_loop(2 * n, 8, add, 0)
        p2_copy(n).start()

    def stage3(n):
        p2_copy(n).wait_recv()
        lanes = pl.ds(n * 256, 256)

        def add(d, carry):
            odd = d % 2
            zz = (z + 4 + (d // 2) * (1 - odd) + (8 - (d + 1) // 2) * odd) % 8

            @pl.when(zz >= 2 * n)
            def _():
                total = s1[zz, xh, :, lanes].astype(F32) + r2[zz, :, lanes].astype(F32)
                s2[zz, :, lanes] = total.astype(BF16)

                @pl.when(zz != z)
                def _():
                    p3_copy(n, zz).start()

                @pl.when(zz == z)
                def _():
                    r3[z, :, lanes] = total.astype(BF16)

            return carry

        lax.fori_loop(0, 8, add, 0)

    def m3_start(d, carry):
        m3_copy(d).start()
        return carry

    def m3_all():
        return remote(rm3.at[pl.ds(0, 7)], rm3.at[pl.ds(0, 7)], m3_s, m3_r, at(zp, xh, c))

    def m4_all():
        return remote(quarters.at[pl.ds(0, 3)], quarters.at[pl.ds(0, 3)], m4_s, m4_r, at(z, xh, oc))

    stage1(3)
    stage1(2)
    mean1.wait_recv()
    mt1[...] = mt0[...] + rm1[...]
    mean2.start()
    stage2(3)
    stage1(1)
    stage2(2)
    stage1(0)
    stage2(1)
    mean2.wait_recv()
    for k in range(4):
        lanes = slice(k * 256, k * 256 + 256)
        mt2[k] = mt1[:, lanes] + rm2[:, lanes]
    rm3[z] = mt2[colour]
    lax.fori_loop(1, 8, m3_start, 0)
    stage2(0)
    stage3(3)
    stage3(2)
    stage3(1)
    stage3(0)
    m3_all().wait_recv()
    grad = rm3[0]
    for p in range(1, 8):
        grad = grad + rm3[p]
    quarters[colour] = grad
    for k in range(3):
        m4_copy(k).start()
    m4_all().wait_recv()
    for k in range(4):
        lanes = slice(k * 256, k * 256 + 256)
        gmean_out[:, lanes] = quarters[k] - m_in[:, lanes].astype(F32)

    def p3_all(n, many):
        lanes = pl.ds(n * 256, 256)
        return remote(
            s2.at[pl.ds(0, many), :, lanes], r3.at[pl.ds(0, many), :, lanes], p3_s.at[n], p3_r.at[n], at(zp, xh, c)
        )

    def p3_wait(n):
        @pl.when(z >= 2 * n)
        def _():
            p3_all(n, 7).wait_recv()

    for n in range(4):
        p3_wait(n)
    data = r3[0].astype(F32)
    for p in range(1, 8):
        data = data + r3[p].astype(F32)
    column_ids = lax.broadcasted_iota(jnp.int32, (32, MB), 1)
    row_ids = lax.broadcasted_iota(jnp.int32, (32, MB), 0) + me * 32
    own_chol = lbuf[z, xh, c].astype(F32)
    on_diag = column_ids == row_ids
    diagonal = jnp.sum(jnp.where(on_diag, own_chol, 0.0), axis=1, keepdims=True)
    gchol_out[...] = (
        jnp.where(column_ids <= row_ids, data, 0.0) - own_chol + jnp.where(on_diag, 1.0 / diagonal, 0.0)
    )

    route_all().wait_send()
    gw.drain()
    gl.drain()

    slot = terms.at[pl.ds(0, 7)]
    remote(slot, slot, st_s, st_r.at[0], (me, (ib + 1) % 8)).wait_send()
    mean1.wait_send()
    mean2.wait_send()
    m3_all().wait_send()
    m4_all().wait_send()
    for n in range(4):
        p1_copy(n).wait_send()
        p2_copy(n).wait_send()

        @pl.when(z >= 2 * n)
        def _():
            p3_all(n, 7 - 2 * n).wait_send()

        @pl.when(z < 2 * n)
        def _():
            p3_all(n, 8 - 2 * n).wait_send()


def body(
    obs_coords, obs_codes, route_plan, inducing_coords, inducing_bands, band_mix, lengthscales,
    class_scales, prior_factor, variational_chol, variational_mean,
):
    vmem = pl.BlockSpec(memory_space=pltpu.VMEM)
    whole = pl.BlockSpec(memory_space=pl.ANY)
    smem = pl.BlockSpec(memory_space=pltpu.SMEM)
    dma = pltpu.SemaphoreType.DMA
    return pl.pallas_call(
        kernel,
        out_shape=(
            pltpu.VMEM((C, ROWS), F32),
            pltpu.VMEM((32, MB), F32),
            pltpu.VMEM((C, MB), F32),
        ),
        in_specs=[whole] * 5 + [smem] * 3 + [whole] * 3,
        out_specs=(vmem, vmem, vmem),
        scratch_shapes=[
            pltpu.VMEM((2, 4096), F32),
            pltpu.VMEM((32, 128), jnp.int32),
            pltpu.VMEM((32, 32), jnp.int32),
            pltpu.VMEM((2, MB), F32),
            pltpu.VMEM((8, 128), jnp.int32),
            pltpu.VMEM((C, MB), BF16),
            dma((8,)),
            pltpu.VMEM((2, 32, 128), F32),
            pltpu.VMEM((32, 4, 128), F32),
            pltpu.VMEM((32, 4, 128), F32),
            pltpu.VMEM((16, 8, 128), F32),
            pltpu.VMEM((8, 2, 256), F32),
            pltpu.VMEM((128, MB), BF16),
            pltpu.VMEM((2, MB), F32),
            pltpu.VMEM((16, MB), BF16),
            pltpu.VMEM((8, 2, 2, 32, MB), BF16),
            pltpu.VMEM((8, 2, 2, 32, MB), BF16),
            pltpu.VMEM((ROWS, MB), BF16),
            pltpu.VMEM((ROWS, MB), BF16),
            pltpu.VMEM((MB, ROWS), BF16),
            pltpu.VMEM((ROWS, MB), F32),
            pltpu.VMEM((ROWS, MB), BF16),
            pltpu.VMEM((ROWS, 128), F32),
            pltpu.VMEM((8, 8, 8, 256), F32),
            pltpu.VMEM((16, ROWS), BF16),
            pltpu.VMEM((8, 2, 2, 32, MB), BF16),
            pltpu.VMEM((8, 2, 32, MB), BF16),
            pltpu.VMEM((8, 2, 32, MB), BF16),
            pltpu.VMEM((8, 32, MB), BF16),
            pltpu.VMEM((8, 32, MB), BF16),
            pltpu.VMEM((8, 32, MB), BF16),
            pltpu.VMEM((8, MB), F32),
            pltpu.VMEM((8, MB), F32),
            pltpu.VMEM((4, 8, 256), F32),
            pltpu.VMEM((8, MB), F32),
            pltpu.VMEM((8, MB), F32),
            pltpu.VMEM((8, 8, 256), F32),
            pltpu.VMEM((4, 8, 256), F32),
            dma(()), dma(()), dma((8,)), dma((16,)), dma((8,)), dma((16,)),
            dma(()), dma((5,)),
            dma((4,)), dma((4,)), dma((4,)), dma((4,)), dma((4,)), dma((4,)),
            dma((2,)), dma((2,)), dma(()), dma(()), dma(()), dma(()),
        ],
        compiler_params=pltpu.CompilerParams(
            collective_id=0, has_side_effects=True, vmem_limit_bytes=60 << 20
        ),
        name="elbo_step",
    )(
        obs_coords, obs_codes.reshape(32, 128), route_plan, inducing_coords,
        inducing_bands.reshape(8, 128), band_mix, lengthscales, class_scales,
        prior_factor, variational_chol, variational_mean,
    )


def solution(mesh):
    placed = (
        P(None, "obs"), P("obs"), P(), P(None, "ind"), P("ind"), P(), P(), P(),
        P(("ind", "obs"), None), P(("ind", "obs"), None), P(None, "ind"),
    )
    return jax.shard_map(
        body,
        mesh=mesh,
        in_specs=placed,
        out_specs=(P(None, "obs"), P(("ind", "obs"), None), P(None, "ind")),
        check_vma=False,
    )
```

```python
import functools
import math

import jax
import jax.numpy as jnp
from jax import lax
from jax.experimental import pallas as pl
from jax.experimental.pallas import tpu as pltpu
from jax.sharding import PartitionSpec as P

C = 8
NB = 6
ROWS = 2048
MB = 1024
MESH = pl.DeviceIdType.MESH
F32 = jnp.float32
BF16 = jnp.bfloat16
ROOT = math.sqrt(0.5 * math.log2(math.e))


def dot_nn(a, b):
    return jnp.dot(a, b, preferred_element_type=F32)


def dot_nt(a, b):
    return lax.dot_general(a, b, (((1,), (1,)), ((), ())), preferred_element_type=F32)


def exact_pick(hot, rows):
    return jnp.dot(hot, rows, precision=lax.Precision.HIGHEST, preferred_element_type=F32)


def kernel(
    coords_in, codes_in, plan_in, centers_in, bands_in, mix_in, ls_in, scales_in,
    w_in, l_in, m_any,
    probs_out, gchol_out, gmean_out,
    coords_ref, codes_ref, plan_ref, centers_ref, bands_ref, m_in, mix_ref, ls_ref, scales_ref, load_sem,
    held, sendbuf, incoming, feat, crow, tab, centers_s, mpad,
    wbuf, lbuf, kbuf, abuf, atbuf, bbuf, hbuf, sq,
    terms, ms,
    gbuf, r1, s1, r2, s2, r3,
    mt0, mt1, mt2, rm1, rm2, rm3, quarters,
    route_s, route_r, agw_s, agw_r, agl_s, agl_r,
    st_s, st_r, p1_s, p1_r, p2_s, p2_r, p3_s, p3_r,
    m12_s, m12_r, m3_s, m3_r, m4_s, m4_r,
):
    me = lax.axis_index("obs")
    ib = lax.axis_index("ind")
    z = me // 4
    xh = (me // 2) % 2
    c = me % 2
    oxh = 1 - xh
    oc = 1 - c
    zp = (z + 1) % 8
    zm = (z + 7) % 8

    def at(zz, xx, cc):
        return (zz * 4 + xx * 2 + cc, ib)

    def remote(src, dst, ssem, rsem, dev):
        return pltpu.make_async_remote_copy(
            src_ref=src, dst_ref=dst, send_sem=ssem, recv_sem=rsem, device_id=dev, device_id_type=MESH
        )

    loads = [
        pltpu.make_async_copy(src, dst, load_sem.at[k])
        for k, (src, dst) in enumerate((
            (coords_in, coords_ref), (codes_in, codes_ref), (plan_in, plan_ref),
            (w_in, wbuf.at[z, xh, c]), (l_in, lbuf.at[z, xh, c]),
            (centers_in, centers_ref), (bands_in, bands_ref), (m_any, m_in),
            (mix_in, mix_ref), (ls_in, ls_ref), (scales_in, scales_ref),
        ))
    ]
    for copy in loads:
        copy.start()
    r3[...] = jnp.zeros_like(r3)

    barrier = pltpu.get_barrier_semaphore()

    def greet_obs(d, carry):
        pl.semaphore_signal(barrier, inc=1, device_id=((me + d) % 32, ib), device_id_type=MESH)
        return carry

    def greet_ind(d, carry):
        pl.semaphore_signal(barrier, inc=1, device_id=(me, (ib + d) % 8), device_id_type=MESH)
        return carry

    lax.fori_loop(1, 32, greet_obs, 0)
    lax.fori_loop(1, 8, greet_ind, 0)

    for copy in loads:
        copy.wait()
    for b in range(32):
        held[0, b : b + 1, :] = coords_ref[0:1, b * 128 : b * 128 + 128]
        held[1, b : b + 1, :] = coords_ref[1:2, b * 128 : b * 128 + 128]
    plan = plan_ref[...]
    sub = lax.broadcasted_iota(jnp.int32, (32, 32), 0)
    lan = lax.broadcasted_iota(jnp.int32, (32, 32), 1)
    plan_row = jnp.sum(jnp.where(sub == me, plan, 0), axis=0, keepdims=True)
    start = jnp.sum(jnp.where(lan < sub, plan_row, 0), axis=1, keepdims=True)
    choose = (lan == start).astype(F32)
    sendbuf[:, 0, :] = exact_pick(choose, held[0])
    sendbuf[:, 1, :] = exact_pick(choose, held[1])
    sendbuf[:, 2, :] = exact_pick(choose, codes_ref[...].astype(F32))
    sendbuf[:, 3, :] = jnp.zeros((32, 128), F32)
    incoming[me] = sendbuf[me]

    pl.semaphore_wait(barrier, 38)

    def route_copy(d):
        peer = (me + d) % 32
        return remote(sendbuf.at[peer], incoming.at[me], route_s, route_r, (peer, ib))

    def route_start(d, carry):
        route_copy(d).start()
        return carry

    class Gather:
        def __init__(self, buf, ss, rs, triangular):
            self.buf, self.ss, self.rs, self.triangular = buf, ss, rs, triangular

        def widths(self, zz, fn):
            if not self.triangular:
                fn(slice(None))
                return
            for v in range(4):

                @pl.when(zz // 2 == v)
                def _():
                    fn(pl.ds(0, (v + 1) * 256))

        def go(self, op, q, j, cc, idx, dev):
            zz = self.unit(q)

            def fn(lanes):
                slot = self.buf.at[zz, j, cc, :, lanes] if self.triangular else self.buf.at[zz, j, cc]
                getattr(remote(slot, slot, self.ss.at[q], self.rs.at[idx], dev), op)()

            self.widths(zz, fn)

        def unit(self, q):
            return (z + (0, 7, 6, 5, 1, 2, 3, 4)[q]) % 8

        def half(self, stream):
            return xh if stream == 0 else oxh

        def along(self, op, stream, q, hops, to):
            idx = 7 * stream + to
            self.go(op, q, self.half(stream), c, idx, at((z + 8 + hops) % 8, xh, c))

        def fourth(self, op):
            for j in range(2):

                @pl.when(xh == j)
                def _():
                    self.along(op, 0, 3 + 3 * j, 1 - 2 * j, 7)

        def core(self, op, stream, q):
            self.go(op, q, self.half(stream), c, 15, at(z, xh, oc))

        def across(self, op, q):
            self.go(op, q, xh, c, 7 + q if q else 0, at(z, oxh, c))

        def wait(self, stream, q):
            idx = 7 * stream + q if q else 0
            self.go("wait_recv", q, self.half(stream), c, idx, at(z, oxh, c))

        def begin(self):
            self.along("start", 0, 0, 1, 1)
            self.along("start", 0, 0, -1, 4)
            self.across("start", 0)
            self.core("start", 0, 0)

        def step(self, stream, k):
            if k == 0:
                self.wait(1, 0)
                self.along("start", 1, 0, 1, 1)
                self.along("start", 1, 0, -1, 4)
                self.core("start", 1, 0)
                return
            if k == 4:
                self.wait(stream, 7)
                if stream == 0:
                    self.across("start", 7)
                self.core("start", stream, 7)
                return
            relay = k < 3 - stream
            self.wait(stream, k)
            if relay:
                self.along("start", stream, k, 1, k + 1)
            self.wait(stream, 3 + k)
            if relay:
                self.along("start", stream, 3 + k, -1, 4 + k)
            if stream == 0 and k == 3:
                self.fourth("start")
                self.across("start", 3)
                self.across("start", 6)
            self.core("start", stream, k)
            self.core("start", stream, 3 + k)

        def end(self):
            rows = pl.ds(0, 320 if self.triangular else 512)
            remote(kbuf.at[rows], abuf.at[rows], self.ss.at[0], self.rs.at[15], at(z, xh, oc)).wait_recv()

        def drain(self):
            for q in range(8):
                many = (7, 4, 3, 3, 4, 3, 3, 3)[q]

                def settle(count):
                    def fn(lanes):
                        rows = pl.ds(0, 32 * count)
                        remote(
                            kbuf.at[rows, lanes], abuf.at[rows, lanes], self.ss.at[q], self.rs.at[15], at(z, xh, oc)
                        ).wait_send()

                    self.widths(self.unit(q), fn)

                if q in (3, 6):
                    pl.when(xh == (q - 3) // 3)(functools.partial(settle, many + 1))
                    pl.when(xh != (q - 3) // 3)(functools.partial(settle, many))
                else:
                    settle(many)

    gw = Gather(wbuf, agw_s, agw_r, False)
    gl = Gather(lbuf, agl_s, agl_r, True)
    gw.begin()
    lax.fori_loop(1, 32, route_start, 0)

    ls0 = jnp.full((1, MB), ls_ref[0], F32)
    ls1 = jnp.full((1, MB), ls_ref[1], F32)
    centers_s[0:1, :] = centers_ref[0:1, :] * (ROOT / ls0)
    centers_s[1:2, :] = centers_ref[1:2, :] * (ROOT / ls1)
    kinds8 = lax.broadcasted_iota(jnp.int32, (8, 128), 0)
    for s in range(8):
        band = jnp.broadcast_to(bands_ref[s : s + 1, :], (8, 128))
        total = (band == kinds8).astype(F32)
        for i in range(NB):
            picked = jnp.zeros((8, 128), F32)
            column = jnp.zeros((8, 128), F32)
            for k in range(NB):
                picked = jnp.where(band == k, mix_ref[k, i], picked)
                column = jnp.where(kinds8 == k, mix_ref[k, i], column)
            total = total + column * picked
        high = total.astype(BF16).astype(F32)
        rest = total - high
        middle = rest.astype(BF16).astype(F32)
        low = rest - middle
        zeros = jnp.zeros((104, 128), F32)
        tab[:, s * 128 : (s + 1) * 128] = jnp.concatenate([high, middle, low, zeros], axis=0).astype(BF16)
    mpad[...] = jnp.concatenate([m_in[...].astype(F32), jnp.zeros((8, MB), F32)], axis=0).astype(BF16)

    plan_col = jnp.sum(jnp.where(lan == me, plan, 0), axis=1, keepdims=True)
    before = jnp.sum(jnp.where(sub < lan, plan_col, 0), axis=0, keepdims=True)
    sub16 = lax.broadcasted_iota(jnp.int32, (16, 32), 0)
    lan16 = lax.broadcasted_iota(jnp.int32, (16, 32), 1)
    source = jnp.sum((before <= sub16).astype(jnp.int32), axis=1, keepdims=True) - 1
    source_hot = (lan16 == source).astype(F32)

    gw.step(0, 1)
    gw.step(1, 0)
    gl.begin()

    def route_all():
        others = pl.ds(0, 31)
        return remote(sendbuf.at[others], incoming.at[others], route_s, route_r, ((me + 1) % 32, ib))

    route_all().wait_recv()

    st = ROOT / jnp.full((1, 128), ls_ref[0], F32)
    sw = ROOT / jnp.full((1, 128), ls_ref[1], F32)
    code = exact_pick(source_hot, incoming[:, 2, :])
    label = jnp.zeros((16, 128), F32)
    for n in range(1, C):
        label = label + (code >= float(NB * n)).astype(F32)
    band = code - float(NB) * label
    feat[:, 0, :] = exact_pick(source_hot, incoming[:, 0, :]) * st
    feat[:, 1, :] = exact_pick(source_hot, incoming[:, 1, :]) * sw
    feat[:, 2, :] = band
    for k in range(3, 8):
        feat[:, k, :] = jnp.zeros((16, 128), F32)
    for k in range(16):
        lanes = slice((k % 2) * 128, (k % 2) * 128 + 128)
        crow[k // 2, 0:1, lanes] = label[k : k + 1, :]
        crow[k // 2, 1:2, lanes] = band[k : k + 1, :]

    lane = lax.broadcasted_iota(jnp.int32, (128, 128), 1)
    kind = (lane % 8).astype(F32)
    live = lane < 24

    def cov_block(b, carry):
        cols = jnp.transpose(feat[b])
        t = cols[:, 0:1]
        w = cols[:, 1:2]
        hot = jnp.where(live & (cols[:, 2:3] == kind), 1.0, 0.0).astype(BF16)
        rows = pl.ds(pl.multiple_of(b * 128, 128), 128)
        for s in range(4):
            lanes = slice(s * 256, s * 256 + 256)
            dt = t - centers_s[0:1, lanes]
            dw = w - centers_s[1:2, lanes]
            mixing = dot_nn(hot, tab[:, lanes])
            kbuf[rows, lanes] = (jnp.exp2(-(dt * dt + dw * dw)) * mixing).astype(BF16)
        return carry

    order = (
        (2, ((gw, 0, 2),)),
        (4, ((gw, 1, 1),)),
        (6, ((gl, 0, 1), (gl, 1, 0))),
        (8, ((gw, 0, 3),)),
        (10, ((gw, 1, 2), (gl, 0, 2))),
        (13, ((gw, 0, 4), (gl, 1, 1))),
        (16, ((gw, 1, 3), (gl, 0, 3), (gw, 1, 4), (gl, 1, 2))),
    )
    done = 0
    for upto, events in order:
        lax.fori_loop(done, upto, cov_block, 0)
        done = upto
        for g, stream, k in events:
            g.step(stream, k)
    gw.end()

    turn = 0
    plan_l = {3: (0, 4), 9: (1, 3), 13: (1, 4)}
    for part in range(4):
        rows = slice(part * 512, part * 512 + 512)
        for n in range(4):
            lanes = slice(n * 256, n * 256 + 256)
            a = dot_nn(kbuf[rows, :], wbuf[:, :, :, :, lanes].reshape(MB, 256))
            abuf[rows, lanes] = a.astype(BF16)
            squares = a[:, :128] * a[:, :128] + a[:, 128:] * a[:, 128:]
            if n == 0:
                sq[rows, :] = squares
            else:
                sq[rows, :] += squares
            if turn in plan_l:
                gl.step(*plan_l[turn])
            turn += 1
    def flip(i, carry):
        rows = pl.ds(pl.multiple_of(i * 256, 256), 256)
        atbuf[:, rows] = jnp.transpose(abuf[rows, :])
        return carry

    gl.end()

    class_ids = lax.broadcasted_iota(jnp.int32, (8, 256), 0)
    scale = jnp.zeros((8, 256), F32)
    for n in range(C):
        scale = jnp.where(class_ids == n, scales_ref[n], scale)

    chunks = ((0, 2), (2, 2), (4, 2), (6, 1), (7, 1))

    def term_slot(src, i):
        first, many = chunks[i]
        return terms.at[src, pl.ds(first, many)]

    def term_copy(i, d):
        slot = term_slot(ib, i)
        return remote(slot, slot, st_s, st_r.at[i], (me, (ib + d) % 8))

    def b_chunk(i):
        first, many = chunks[i]
        lo, size = first * 256, many * 256
        rows = slice(lo, lo + size)
        squares = -sq[rows, :]
        for n in range(4):
            lanes = slice(n * 256, n * 256 + 256)
            deep = slice(n * 256, MB)
            lower = lbuf[2 * n :, :, :, :, lanes].reshape(MB - n * 256, 256)
            b = dot_nn(abuf[rows, deep], lower)
            bbuf[rows, lanes] = b
            squares = squares + (b[:, :128] * b[:, :128] + b[:, 128:] * b[:, 128:])
        means = dot_nt(mpad[...], abuf[rows, :])[0:8, :]
        var = jnp.sum(jnp.transpose(squares), axis=0, keepdims=True)
        for k in range(many):
            lanes = slice(k * 256, k * 256 + 256)
            terms[ib, first + k] = means[:, lanes] + 0.5 * scale * var[:, lanes]

        def send(d, carry):
            term_copy(i, d).start()
            return carry

        lax.fori_loop(1, 8, send, 0)

    for i in range(5):
        b_chunk(i)

    def term_wait(i):
        first, many = chunks[i]
        slot = terms.at[pl.ds(0, 7), pl.ds(first, many)]
        remote(slot, slot, st_s, st_r.at[i], (me, (ib + 1) % 8)).wait_recv()

    values = []
    for k in range(NB):
        value = jnp.float32(1.0)
        for i in range(NB):
            value = value + mix_ref[k, i] * mix_ref[k, i]
        values.append(value)
    classes = class_ids.astype(F32)

    def likelihood(p):
        lanes = slice(p * 256, p * 256 + 256)
        logits = terms[0, p]
        for q in range(1, 8):
            logits = logits + terms[q, p]
        band = crow[p, 1:2, :]
        own = jnp.zeros((1, 256), F32)
        for k in range(NB):
            own = jnp.where(band == float(k), values[k], own)
        weights = jnp.exp(logits + 0.5 * scale * own)
        ch = weights / jnp.sum(weights, axis=0, keepdims=True)
        probs_out[:, lanes] = ch
        slope = jnp.where(crow[p, 0:1, :] == classes, 1.0, 0.0) - ch
        ms[:, lanes] = jnp.concatenate([slope, jnp.zeros((8, 256), F32)], axis=0).astype(BF16)
        slope = -jnp.sum(ch * scale, axis=0, keepdims=True)
        column = jnp.transpose(jnp.broadcast_to(slope, (8, 256)))[:, 0:1]
        rows = slice(p * 256, p * 256 + 256)
        hbuf[rows, :] = (column * bbuf[rows, :]).astype(BF16)

    lax.fori_loop(0, 8, flip, 0)
    term_wait(0)
    term_wait(1)
    for p in range(4):
        likelihood(p)
    mt0[...] = dot_nn(ms[:, 0:1024], abuf[0:1024, :])[0:8, :]
    for n in range(4):
        lanes = slice(n * 256, n * 256 + 256)
        for lo in range(n * 256, MB, 512):
            hi = min(lo + 512, MB)
            bbuf[lo:hi, lanes] = dot_nn(atbuf[lo:hi, 0:1024], hbuf[0:1024, lanes])
    for i in range(2, 5):
        term_wait(i)
    for p in range(4, 8):
        likelihood(p)

    mt0[...] += dot_nn(ms[:, 1024:2048], abuf[1024:2048, :])[0:8, :]
    mean1 = remote(mt0, rm1, m12_s.at[0], m12_r.at[0], at(z, xh, oc))
    mean1.start()

    colour = xh * 2 + c

    def m3_copy(d):
        return remote(mt2.at[colour], rm3.at[z], m3_s, m3_r, at((z + d) % 8, xh, c))

    def m4_copy(k):
        dev = (at(z, xh, oc), at(z, oxh, c), at(z, oxh, oc))[k]
        return remote(quarters.at[colour], quarters.at[colour], m4_s, m4_r, dev)

    mean2 = remote(mt1, rm2, m12_s.at[1], m12_r.at[1], at(z, oxh, c))

    def p1_copy(n):
        lanes = pl.ds(n * 256, 256)
        return remote(
            gbuf.at[pl.ds(2 * n, 8 - 2 * n), :, oc, :, lanes],
            r1.at[pl.ds(2 * n, 8 - 2 * n), :, :, lanes],
            p1_s.at[n], p1_r.at[n], at(z, xh, oc),
        )

    def p2_copy(n):
        lanes = pl.ds(n * 256, 256)
        return remote(
            s1.at[pl.ds(2 * n, 8 - 2 * n), oxh, :, lanes],
            r2.at[pl.ds(2 * n, 8 - 2 * n), :, lanes],
            p2_s.at[n], p2_r.at[n], at(z, oxh, c),
        )

    def p3_copy(n, zz):
        lanes = pl.ds(n * 256, 256)
        return remote(
            s2.at[zz, :, lanes], r3.at[z, :, lanes], p3_s.at[n], p3_r.at[n], at(zz, xh, c)
        )

    def stage1(n):
        lanes = slice(n * 256, n * 256 + 256)
        for lo in range(n * 256, MB, 512):
            hi = min(lo + 512, MB)
            g = dot_nn(atbuf[lo:hi, 1024:2048], hbuf[1024:2048, lanes])
            g = (g + bbuf[lo:hi, lanes]).astype(BF16)
            gbuf[lo // 128 : hi // 128, :, :, :, lanes] = g.reshape((hi - lo) // 128, 2, 2, 32, 256)
        p1_copy(n).start()

    def stage2(n):
        p1_copy(n).wait_recv()
        lanes = pl.ds(n * 256, 256)

        def add(zz, carry):
            for j in range(2):
                total = gbuf[zz, j, c, :, lanes].astype(F32) + r1[zz, j, :, lanes].astype(F32)
                s1[zz, j, :, lanes] = total.astype(BF16)
            return carry

        lax.fori_loop(2 * n, 8, add, 0)
        p2_copy(n).start()

    def stage3(n):
        p2_copy(n).wait_recv()
        lanes = pl.ds(n * 256, 256)

        def add(d, carry):
            odd = d % 2
            zz = (z + 4 + (d // 2) * (1 - odd) + (8 - (d + 1) // 2) * odd) % 8

            @pl.when(zz >= 2 * n)
            def _():
                total = s1[zz, xh, :, lanes].astype(F32) + r2[zz, :, lanes].astype(F32)
                s2[zz, :, lanes] = total.astype(BF16)

                @pl.when(zz != z)
                def _():
                    p3_copy(n, zz).start()

                @pl.when(zz == z)
                def _():
                    r3[z, :, lanes] = total.astype(BF16)

            return carry

        lax.fori_loop(0, 8, add, 0)

    def m3_start(d, carry):
        m3_copy(d).start()
        return carry

    def m3_all():
        return remote(rm3.at[pl.ds(0, 7)], rm3.at[pl.ds(0, 7)], m3_s, m3_r, at(zp, xh, c))

    def m4_all():
        return remote(quarters.at[pl.ds(0, 3)], quarters.at[pl.ds(0, 3)], m4_s, m4_r, at(z, xh, oc))

    stage1(3)
    stage1(2)
    mean1.wait_recv()
    mt1[...] = mt0[...] + rm1[...]
    mean2.start()
    stage2(3)
    stage1(1)
    stage2(2)
    stage1(0)
    stage2(1)
    mean2.wait_recv()
    for k in range(4):
        lanes = slice(k * 256, k * 256 + 256)
        mt2[k] = mt1[:, lanes] + rm2[:, lanes]
    rm3[z] = mt2[colour]
    lax.fori_loop(1, 8, m3_start, 0)
    stage2(0)
    stage3(3)
    stage3(2)
    stage3(1)
    stage3(0)
    m3_all().wait_recv()
    grad = rm3[0]
    for p in range(1, 8):
        grad = grad + rm3[p]
    quarters[colour] = grad
    for k in range(3):
        m4_copy(k).start()
    m4_all().wait_recv()
    for k in range(4):
        lanes = slice(k * 256, k * 256 + 256)
        gmean_out[:, lanes] = quarters[k] - m_in[:, lanes].astype(F32)

    def p3_all(n, many):
        lanes = pl.ds(n * 256, 256)
        return remote(
            s2.at[pl.ds(0, many), :, lanes], r3.at[pl.ds(0, many), :, lanes], p3_s.at[n], p3_r.at[n], at(zp, xh, c)
        )

    def p3_wait(n):
        @pl.when(z >= 2 * n)
        def _():
            p3_all(n, 7).wait_recv()

    for n in range(4):
        p3_wait(n)
    data = r3[0].astype(F32)
    for p in range(1, 8):
        data = data + r3[p].astype(F32)
    column_ids = lax.broadcasted_iota(jnp.int32, (32, MB), 1)
    row_ids = lax.broadcasted_iota(jnp.int32, (32, MB), 0) + me * 32
    own_chol = lbuf[z, xh, c].astype(F32)
    on_diag = column_ids == row_ids
    diagonal = jnp.sum(jnp.where(on_diag, own_chol, 0.0), axis=1, keepdims=True)
    gchol_out[...] = (
        jnp.where(column_ids <= row_ids, data, 0.0) - own_chol + jnp.where(on_diag, 1.0 / diagonal, 0.0)
    )

    route_all().wait_send()
    gw.drain()
    gl.drain()

    slot = terms.at[pl.ds(0, 7)]
    remote(slot, slot, st_s, st_r.at[0], (me, (ib + 1) % 8)).wait_send()
    mean1.wait_send()
    mean2.wait_send()
    m3_all().wait_send()
    m4_all().wait_send()
    for n in range(4):
        p1_copy(n).wait_send()
        p2_copy(n).wait_send()

        @pl.when(z >= 2 * n)
        def _():
            p3_all(n, 7 - 2 * n).wait_send()

        @pl.when(z < 2 * n)
        def _():
            p3_all(n, 8 - 2 * n).wait_send()


def body(
    obs_coords, obs_codes, route_plan, inducing_coords, inducing_bands, band_mix, lengthscales,
    class_scales, prior_factor, variational_chol, variational_mean,
):
    vmem = pl.BlockSpec(memory_space=pltpu.VMEM)
    whole = pl.BlockSpec(memory_space=pl.ANY)
    dma = pltpu.SemaphoreType.DMA
    return pl.pallas_call(
        kernel,
        out_shape=(
            pltpu.VMEM((C, ROWS), F32),
            pltpu.VMEM((32, MB), F32),
            pltpu.VMEM((C, MB), F32),
        ),
        in_specs=[whole] * 11,
        out_specs=(vmem, vmem, vmem),
        scratch_shapes=[
            pltpu.VMEM((2, 4096), F32),
            pltpu.VMEM((32, 128), jnp.int32),
            pltpu.VMEM((32, 32), jnp.int32),
            pltpu.VMEM((2, MB), F32),
            pltpu.VMEM((8, 128), jnp.int32),
            pltpu.VMEM((C, MB), BF16),
            pltpu.SMEM((NB, NB), F32), pltpu.SMEM((2,), F32), pltpu.SMEM((C,), F32),
            dma((11,)),
            pltpu.VMEM((2, 32, 128), F32),
            pltpu.VMEM((32, 4, 128), F32),
            pltpu.VMEM((32, 4, 128), F32),
            pltpu.VMEM((16, 8, 128), F32),
            pltpu.VMEM((8, 2, 256), F32),
            pltpu.VMEM((128, MB), BF16),
            pltpu.VMEM((2, MB), F32),
            pltpu.VMEM((16, MB), BF16),
            pltpu.VMEM((8, 2, 2, 32, MB), BF16),
            pltpu.VMEM((8, 2, 2, 32, MB), BF16),
            pltpu.VMEM((ROWS, MB), BF16),
            pltpu.VMEM((ROWS, MB), BF16),
            pltpu.VMEM((MB, ROWS), BF16),
            pltpu.VMEM((ROWS, MB), F32),
            pltpu.VMEM((ROWS, MB), BF16),
            pltpu.VMEM((ROWS, 128), F32),
            pltpu.VMEM((8, 8, 8, 256), F32),
            pltpu.VMEM((16, ROWS), BF16),
            pltpu.VMEM((8, 2, 2, 32, MB), BF16),
            pltpu.VMEM((8, 2, 32, MB), BF16),
            pltpu.VMEM((8, 2, 32, MB), BF16),
            pltpu.VMEM((8, 32, MB), BF16),
            pltpu.VMEM((8, 32, MB), BF16),
            pltpu.VMEM((8, 32, MB), BF16),
            pltpu.VMEM((8, MB), F32),
            pltpu.VMEM((8, MB), F32),
            pltpu.VMEM((4, 8, 256), F32),
            pltpu.VMEM((8, MB), F32),
            pltpu.VMEM((8, MB), F32),
            pltpu.VMEM((8, 8, 256), F32),
            pltpu.VMEM((4, 8, 256), F32),
            dma(()), dma(()), dma((8,)), dma((16,)), dma((8,)), dma((16,)),
            dma(()), dma((5,)),
            dma((4,)), dma((4,)), dma((4,)), dma((4,)), dma((4,)), dma((4,)),
            dma((2,)), dma((2,)), dma(()), dma(()), dma(()), dma(()),
        ],
        compiler_params=pltpu.CompilerParams(
            collective_id=0, has_side_effects=True, vmem_limit_bytes=60 << 20
        ),
        name="elbo_step",
    )(
        obs_coords, obs_codes.reshape(32, 128), route_plan, inducing_coords,
        inducing_bands.reshape(8, 128), band_mix, lengthscales, class_scales,
        prior_factor, variational_chol, variational_mean,
    )


def solution(mesh):
    placed = (
        P(None, "obs"), P("obs"), P(), P(None, "ind"), P("ind"), P(), P(), P(),
        P(("ind", "obs"), None), P(("ind", "obs"), None), P(None, "ind"),
    )
    return jax.shard_map(
        body,
        mesh=mesh,
        in_specs=placed,
        out_specs=(P(None, "obs"), P(("ind", "obs"), None), P(None, "ind")),
        check_vma=False,
    )
```

```python
import functools
import math

import jax
import jax.numpy as jnp
from jax import lax
from jax.experimental import pallas as pl
from jax.experimental.pallas import tpu as pltpu
from jax.sharding import PartitionSpec as P

C = 8
NB = 6
ROWS = 2048
MB = 1024
MESH = pl.DeviceIdType.MESH
F32 = jnp.float32
BF16 = jnp.bfloat16
ROOT = math.sqrt(0.5 * math.log2(math.e))


def dot_nn(a, b):
    return jnp.dot(a, b, preferred_element_type=F32)


def dot_nt(a, b):
    return lax.dot_general(a, b, (((1,), (1,)), ((), ())), preferred_element_type=F32)


def exact_pick(hot, rows):
    return jnp.dot(hot, rows, precision=lax.Precision.HIGHEST, preferred_element_type=F32)


def kernel(
    coords_in, codes_in, plan_in, centers_in, bands_in, mix_in, ls_in, scales_in,
    w_in, l_in, m_any,
    probs_out, gchol_out, gmean_out,
    coords_ref, codes_ref, plan_ref, centers_ref, bands_ref, m_in, mix_ref, ls_ref, scales_ref, load_sem,
    held, sendbuf, incoming, feat, crow, tab, centers_s, mpad,
    wbuf, lbuf, kbuf, abuf, atbuf, bbuf, hbuf, sq,
    terms, ms,
    gbuf, r1, s1, r2, s2, r3,
    mt0, mt1, mt2, rm1, rm2, rm3, quarters,
    route_s, route_r, agw_s, agw_r, agl_s, agl_r,
    st_s, st_r, p1_s, p1_r, p2_s, p2_r, p3_s, p3_r,
    m12_s, m12_r, m3_s, m3_r, m4_s, m4_r,
):
    me = lax.axis_index("obs")
    ib = lax.axis_index("ind")
    z = me // 4
    xh = (me // 2) % 2
    c = me % 2
    oxh = 1 - xh
    oc = 1 - c
    zp = (z + 1) % 8
    zm = (z + 7) % 8

    def at(zz, xx, cc):
        return (zz * 4 + xx * 2 + cc, ib)

    def remote(src, dst, ssem, rsem, dev):
        return pltpu.make_async_remote_copy(
            src_ref=src, dst_ref=dst, send_sem=ssem, recv_sem=rsem, device_id=dev, device_id_type=MESH
        )

    loads = [
        pltpu.make_async_copy(src, dst, load_sem.at[k])
        for k, (src, dst) in enumerate((
            (coords_in, coords_ref), (codes_in, codes_ref), (plan_in, plan_ref),
            (w_in, wbuf.at[z, xh, c]), (l_in, lbuf.at[z, xh, c]),
            (centers_in, centers_ref), (bands_in, bands_ref), (m_any, m_in),
            (mix_in, mix_ref), (ls_in, ls_ref), (scales_in, scales_ref),
        ))
    ]
    for copy in loads:
        copy.start()
    r3[...] = jnp.zeros_like(r3)

    barrier = pltpu.get_barrier_semaphore()

    def greet_obs(d, carry):
        pl.semaphore_signal(barrier, inc=1, device_id=((me + d) % 32, ib), device_id_type=MESH)
        return carry

    def greet_ind(d, carry):
        pl.semaphore_signal(barrier, inc=1, device_id=(me, (ib + d) % 8), device_id_type=MESH)
        return carry

    lax.fori_loop(1, 32, greet_obs, 0)
    lax.fori_loop(1, 8, greet_ind, 0)

    for copy in loads:
        copy.wait()
    for b in range(32):
        held[0, b : b + 1, :] = coords_ref[0:1, b * 128 : b * 128 + 128]
        held[1, b : b + 1, :] = coords_ref[1:2, b * 128 : b * 128 + 128]
    plan = plan_ref[...]
    sub = lax.broadcasted_iota(jnp.int32, (32, 32), 0)
    lan = lax.broadcasted_iota(jnp.int32, (32, 32), 1)
    plan_row = jnp.sum(jnp.where(sub == me, plan, 0), axis=0, keepdims=True)
    start = jnp.sum(jnp.where(lan < sub, plan_row, 0), axis=1, keepdims=True)
    choose = (lan == start).astype(F32)
    sendbuf[:, 0, :] = exact_pick(choose, held[0])
    sendbuf[:, 1, :] = exact_pick(choose, held[1])
    sendbuf[:, 2, :] = exact_pick(choose, codes_ref[...].astype(F32))
    sendbuf[:, 3, :] = jnp.zeros((32, 128), F32)
    incoming[me] = sendbuf[me]

    pl.semaphore_wait(barrier, 38)

    def route_copy(d):
        peer = (me + d) % 32
        return remote(sendbuf.at[peer], incoming.at[me], route_s, route_r, (peer, ib))

    def route_start(d, carry):
        route_copy(d).start()
        return carry

    class Gather:
        def __init__(self, buf, ss, rs, triangular):
            self.buf, self.ss, self.rs, self.triangular = buf, ss, rs, triangular

        def widths(self, zz, fn):
            if not self.triangular:
                fn(slice(None))
                return
            for v in range(4):

                @pl.when(zz // 2 == v)
                def _():
                    fn(pl.ds(0, (v + 1) * 256))

        def go(self, op, q, j, cc, idx, dev):
            zz = self.unit(q)

            def fn(lanes):
                slot = self.buf.at[zz, j, cc, :, lanes] if self.triangular else self.buf.at[zz, j, cc]
                getattr(remote(slot, slot, self.ss.at[q], self.rs.at[idx], dev), op)()

            self.widths(zz, fn)

        def unit(self, q):
            return (z + (0, 7, 6, 5, 1, 2, 3, 4)[q]) % 8

        def half(self, stream):
            return xh if stream == 0 else oxh

        def along(self, op, stream, q, hops, to):
            idx = 7 * stream + to
            self.go(op, q, self.half(stream), c, idx, at((z + 8 + hops) % 8, xh, c))

        def fourth(self, op):
            for j in range(2):

                @pl.when(xh == j)
                def _():
                    self.along(op, 0, 3 + 3 * j, 1 - 2 * j, 7)

        def core(self, op, stream, q):
            self.go(op, q, self.half(stream), c, 15, at(z, xh, oc))

        def across(self, op, q):
            self.go(op, q, xh, c, 7 + q if q else 0, at(z, oxh, c))

        def wait(self, stream, q):
            idx = 7 * stream + q if q else 0
            self.go("wait_recv", q, self.half(stream), c, idx, at(z, oxh, c))

        def begin(self):
            self.along("start", 0, 0, 1, 1)
            self.along("start", 0, 0, -1, 4)
            self.across("start", 0)
            self.core("start", 0, 0)

        def step(self, stream, k):
            if k == 0:
                self.wait(1, 0)
                self.along("start", 1, 0, 1, 1)
                self.along("start", 1, 0, -1, 4)
                self.core("start", 1, 0)
                return
            if k == 4:
                self.wait(stream, 7)
                if stream == 0:
                    self.across("start", 7)
                self.core("start", stream, 7)
                return
            relay = k < 3 - stream
            self.wait(stream, k)
            if relay:
                self.along("start", stream, k, 1, k + 1)
            self.wait(stream, 3 + k)
            if relay:
                self.along("start", stream, 3 + k, -1, 4 + k)
            if stream == 0 and k == 3:
                self.fourth("start")
                self.across("start", 3)
                self.across("start", 6)
            self.core("start", stream, k)
            self.core("start", stream, 3 + k)

        def end(self):
            rows = pl.ds(0, 320 if self.triangular else 512)
            remote(kbuf.at[rows], abuf.at[rows], self.ss.at[0], self.rs.at[15], at(z, xh, oc)).wait_recv()

        def drain(self):
            for q in range(8):
                many = (7, 4, 3, 3, 4, 3, 3, 3)[q]

                def settle(count):
                    def fn(lanes):
                        rows = pl.ds(0, 32 * count)
                        remote(
                            kbuf.at[rows, lanes], abuf.at[rows, lanes], self.ss.at[q], self.rs.at[15], at(z, xh, oc)
                        ).wait_send()

                    self.widths(self.unit(q), fn)

                if q in (3, 6):
                    pl.when(xh == (q - 3) // 3)(functools.partial(settle, many + 1))
                    pl.when(xh != (q - 3) // 3)(functools.partial(settle, many))
                else:
                    settle(many)

    gw = Gather(wbuf, agw_s, agw_r, False)
    gl = Gather(lbuf, agl_s, agl_r, True)
    gw.begin()
    lax.fori_loop(1, 32, route_start, 0)

    ls0 = jnp.full((1, MB), ls_ref[0], F32)
    ls1 = jnp.full((1, MB), ls_ref[1], F32)
    centers_s[0:1, :] = centers_ref[0:1, :] * (ROOT / ls0)
    centers_s[1:2, :] = centers_ref[1:2, :] * (ROOT / ls1)
    kinds8 = lax.broadcasted_iota(jnp.int32, (8, 128), 0)
    for s in range(8):
        band = jnp.broadcast_to(bands_ref[s : s + 1, :], (8, 128))
        total = (band == kinds8).astype(F32)
        for i in range(NB):
            picked = jnp.zeros((8, 128), F32)
            column = jnp.zeros((8, 128), F32)
            for k in range(NB):
                picked = jnp.where(band == k, mix_ref[k, i], picked)
                column = jnp.where(kinds8 == k, mix_ref[k, i], column)
            total = total + column * picked
        high = total.astype(BF16).astype(F32)
        rest = total - high
        middle = rest.astype(BF16).astype(F32)
        low = rest - middle
        zeros = jnp.zeros((104, 128), F32)
        tab[:, s * 128 : (s + 1) * 128] = jnp.concatenate([high, middle, low, zeros], axis=0).astype(BF16)
    mpad[...] = jnp.concatenate([m_in[...].astype(F32), jnp.zeros((8, MB), F32)], axis=0).astype(BF16)

    plan_col = jnp.sum(jnp.where(lan == me, plan, 0), axis=1, keepdims=True)
    before = jnp.sum(jnp.where(sub < lan, plan_col, 0), axis=0, keepdims=True)
    sub16 = lax.broadcasted_iota(jnp.int32, (16, 32), 0)
    lan16 = lax.broadcasted_iota(jnp.int32, (16, 32), 1)
    source = jnp.sum((before <= sub16).astype(jnp.int32), axis=1, keepdims=True) - 1
    source_hot = (lan16 == source).astype(F32)

    gw.step(0, 1)
    gw.step(1, 0)
    gl.begin()

    def route_all():
        others = pl.ds(0, 31)
        return remote(sendbuf.at[others], incoming.at[others], route_s, route_r, ((me + 1) % 32, ib))

    route_all().wait_recv()

    st = ROOT / jnp.full((1, 128), ls_ref[0], F32)
    sw = ROOT / jnp.full((1, 128), ls_ref[1], F32)
    code = exact_pick(source_hot, incoming[:, 2, :])
    label = jnp.zeros((16, 128), F32)
    for n in range(1, C):
        label = label + (code >= float(NB * n)).astype(F32)
    band = code - float(NB) * label
    feat[:, 0, :] = exact_pick(source_hot, incoming[:, 0, :]) * st
    feat[:, 1, :] = exact_pick(source_hot, incoming[:, 1, :]) * sw
    feat[:, 2, :] = band
    for k in range(3, 8):
        feat[:, k, :] = jnp.zeros((16, 128), F32)
    for k in range(16):
        lanes = slice((k % 2) * 128, (k % 2) * 128 + 128)
        crow[k // 2, 0:1, lanes] = label[k : k + 1, :]
        crow[k // 2, 1:2, lanes] = band[k : k + 1, :]

    lane = lax.broadcasted_iota(jnp.int32, (128, 128), 1)
    kind = (lane % 8).astype(F32)
    live = lane < 24

    def cov_block(b, carry):
        cols = jnp.transpose(feat[b])
        t = cols[:, 0:1]
        w = cols[:, 1:2]
        hot = jnp.where(live & (cols[:, 2:3] == kind), 1.0, 0.0).astype(BF16)
        rows = pl.ds(pl.multiple_of(b * 128, 128), 128)
        for s in range(4):
            lanes = slice(s * 256, s * 256 + 256)
            dt = t - centers_s[0:1, lanes]
            dw = w - centers_s[1:2, lanes]
            mixing = dot_nn(hot, tab[:, lanes])
            kbuf[rows, lanes] = (jnp.exp2(-(dt * dt + dw * dw)) * mixing).astype(BF16)
        return carry

    order = (
        (2, ((gw, 0, 2),)),
        (4, ((gw, 1, 1),)),
        (6, ((gl, 0, 1), (gl, 1, 0))),
        (8, ((gw, 0, 3),)),
        (10, ((gw, 1, 2), (gl, 0, 2))),
        (13, ((gw, 0, 4), (gl, 1, 1))),
        (16, ((gw, 1, 3), (gl, 0, 3), (gw, 1, 4), (gl, 1, 2))),
    )
    done = 0
    for upto, events in order:
        lax.fori_loop(done, upto, cov_block, 0)
        done = upto
        for g, stream, k in events:
            g.step(stream, k)
    gw.end()

    turn = 0
    plan_l = {3: (0, 4), 9: (1, 3), 13: (1, 4)}
    for part in range(4):
        rows = slice(part * 512, part * 512 + 512)
        for n in range(4):
            lanes = slice(n * 256, n * 256 + 256)
            a = dot_nn(kbuf[rows, :], wbuf[:, :, :, :, lanes].reshape(MB, 256))
            abuf[rows, lanes] = a.astype(BF16)
            squares = a[:, :128] * a[:, :128] + a[:, 128:] * a[:, 128:]
            if n == 0:
                sq[rows, :] = squares
            else:
                sq[rows, :] += squares
            if turn in plan_l:
                gl.step(*plan_l[turn])
            turn += 1
    def flip(i, carry):
        rows = pl.ds(pl.multiple_of(i * 256, 256), 256)
        atbuf[:, rows] = jnp.transpose(abuf[rows, :])
        return carry

    gl.end()

    class_ids = lax.broadcasted_iota(jnp.int32, (8, 256), 0)
    scale = jnp.zeros((8, 256), F32)
    for n in range(C):
        scale = jnp.where(class_ids == n, scales_ref[n], scale)

    chunks = ((0, 2), (2, 2), (4, 2), (6, 1), (7, 1))

    def term_slot(src, i):
        first, many = chunks[i]
        return terms.at[src, pl.ds(first, many)]

    def term_copy(i, d):
        slot = term_slot(ib, i)
        return remote(slot, slot, st_s, st_r.at[i], (me, (ib + d) % 8))

    def b_chunk(i):
        first, many = chunks[i]
        lo, size = first * 256, many * 256
        rows = slice(lo, lo + size)
        squares = -sq[rows, :]
        for n in range(4):
            lanes = slice(n * 256, n * 256 + 256)
            deep = slice(n * 256, MB)
            lower = lbuf[2 * n :, :, :, :, lanes].reshape(MB - n * 256, 256)
            b = dot_nn(abuf[rows, deep], lower)
            bbuf[rows, lanes] = b
            squares = squares + (b[:, :128] * b[:, :128] + b[:, 128:] * b[:, 128:])
        means = dot_nt(mpad[...], abuf[rows, :])[0:8, :]
        var = jnp.sum(jnp.transpose(squares), axis=0, keepdims=True)
        for k in range(many):
            lanes = slice(k * 256, k * 256 + 256)
            terms[ib, first + k] = means[:, lanes] + 0.5 * scale * var[:, lanes]

        def send(d, carry):
            term_copy(i, d).start()
            return carry

        lax.fori_loop(1, 8, send, 0)

    for i in range(5):
        b_chunk(i)

    def term_wait(i):
        first, many = chunks[i]
        slot = terms.at[pl.ds(0, 7), pl.ds(first, many)]
        remote(slot, slot, st_s, st_r.at[i], (me, (ib + 1) % 8)).wait_recv()

    values = []
    for k in range(NB):
        value = jnp.float32(1.0)
        for i in range(NB):
            value = value + mix_ref[k, i] * mix_ref[k, i]
        values.append(value)
    classes = class_ids.astype(F32)

    def likelihood(p):
        lanes = slice(p * 256, p * 256 + 256)
        logits = terms[0, p]
        for q in range(1, 8):
            logits = logits + terms[q, p]
        band = crow[p, 1:2, :]
        own = jnp.zeros((1, 256), F32)
        for k in range(NB):
            own = jnp.where(band == float(k), values[k], own)
        weights = jnp.exp(logits + 0.5 * scale * own)
        ch = weights / jnp.sum(weights, axis=0, keepdims=True)
        probs_out[:, lanes] = ch
        slope = jnp.where(crow[p, 0:1, :] == classes, 1.0, 0.0) - ch
        ms[:, lanes] = jnp.concatenate([slope, jnp.zeros((8, 256), F32)], axis=0).astype(BF16)
        slope = -jnp.sum(ch * scale, axis=0, keepdims=True)
        column = jnp.transpose(jnp.broadcast_to(slope, (8, 256)))[:, 0:1]
        rows = slice(p * 256, p * 256 + 256)
        hbuf[rows, :] = (column * bbuf[rows, :]).astype(BF16)

    lax.fori_loop(0, 8, flip, 0)
    term_wait(0)
    term_wait(1)
    for p in range(4):
        likelihood(p)
    mt0[...] = dot_nn(ms[:, 0:1024], abuf[0:1024, :])[0:8, :]
    for n in range(4):
        lanes = slice(n * 256, n * 256 + 256)
        for lo in range(n * 256, MB, 512):
            hi = min(lo + 512, MB)
            bbuf[lo:hi, lanes] = dot_nn(atbuf[lo:hi, 0:1024], hbuf[0:1024, lanes])
    for i in range(2, 5):
        term_wait(i)
    for p in range(4, 8):
        likelihood(p)

    mt0[...] += dot_nn(ms[:, 1024:2048], abuf[1024:2048, :])[0:8, :]
    mean1 = remote(mt0, rm1, m12_s.at[0], m12_r.at[0], at(z, xh, oc))
    mean1.start()

    colour = xh * 2 + c

    def m3_copy(d):
        return remote(mt2.at[colour], rm3.at[z], m3_s, m3_r, at((z + d) % 8, xh, c))

    def m4_copy(k):
        dev = (at(z, xh, oc), at(z, oxh, c), at(z, oxh, oc))[k]
        return remote(quarters.at[colour], quarters.at[colour], m4_s, m4_r, dev)

    mean2 = remote(mt1, rm2, m12_s.at[1], m12_r.at[1], at(z, oxh, c))

    def p1_copy(n):
        lanes = pl.ds(n * 256, 256)
        return remote(
            gbuf.at[pl.ds(2 * n, 8 - 2 * n), :, oc, :, lanes],
            r1.at[pl.ds(2 * n, 8 - 2 * n), :, :, lanes],
            p1_s.at[n], p1_r.at[n], at(z, xh, oc),
        )

    parts = ((0, 128), (256, 256), (512, 256), (768, 256), (128, 128))
    firsts = (0, 2, 4, 6, 0)

    def p2_copy(n):
        lanes = pl.ds(*parts[n])
        return remote(
            s1.at[pl.ds(firsts[n], 8 - firsts[n]), oxh, :, lanes],
            r2.at[pl.ds(firsts[n], 8 - firsts[n]), :, lanes],
            p2_s.at[n], p2_r.at[n], at(z, oxh, c),
        )

    def p3_copy(n, zz):
        lanes = pl.ds(*parts[n])
        return remote(
            s2.at[zz, :, lanes], r3.at[z, :, lanes], p3_s.at[n], p3_r.at[n], at(zz, xh, c)
        )

    def stage1(n):
        lanes = slice(n * 256, n * 256 + 256)
        for lo in range(n * 256, MB, 512):
            hi = min(lo + 512, MB)
            g = dot_nn(atbuf[lo:hi, 1024:2048], hbuf[1024:2048, lanes])
            g = (g + bbuf[lo:hi, lanes]).astype(BF16)
            gbuf[lo // 128 : hi // 128, :, :, :, lanes] = g.reshape((hi - lo) // 128, 2, 2, 32, 256)
        p1_copy(n).start()

    def stage2(n):
        p1_copy(n).wait_recv()
        for part in (0, 4) if n == 0 else (n,):
            lanes = pl.ds(*parts[part])

            def add(zz, carry):
                for j in range(2):
                    total = gbuf[zz, j, c, :, lanes].astype(F32) + r1[zz, j, :, lanes].astype(F32)
                    s1[zz, j, :, lanes] = total.astype(BF16)
                return carry

            lax.fori_loop(2 * n, 8, add, 0)
            p2_copy(part).start()

    def stage3(n):
        p2_copy(n).wait_recv()
        lanes = pl.ds(*parts[n])

        def add(d, carry):
            odd = d % 2
            zz = (z + 4 + (d // 2) * (1 - odd) + (8 - (d + 1) // 2) * odd) % 8

            @pl.when(zz >= firsts[n])
            def _():
                total = s1[zz, xh, :, lanes].astype(F32) + r2[zz, :, lanes].astype(F32)
                s2[zz, :, lanes] = total.astype(BF16)

                @pl.when(zz != z)
                def _():
                    p3_copy(n, zz).start()

                @pl.when(zz == z)
                def _():
                    r3[z, :, lanes] = total.astype(BF16)

            return carry

        lax.fori_loop(0, 8, add, 0)

    def m3_start(d, carry):
        m3_copy(d).start()
        return carry

    def m3_all():
        return remote(rm3.at[pl.ds(0, 7)], rm3.at[pl.ds(0, 7)], m3_s, m3_r, at(zp, xh, c))

    def m4_all():
        return remote(quarters.at[pl.ds(0, 3)], quarters.at[pl.ds(0, 3)], m4_s, m4_r, at(z, xh, oc))

    stage1(3)
    stage1(2)
    mean1.wait_recv()
    mt1[...] = mt0[...] + rm1[...]
    mean2.start()
    stage2(3)
    stage1(1)
    stage2(2)
    stage1(0)
    stage2(1)
    mean2.wait_recv()
    for k in range(4):
        lanes = slice(k * 256, k * 256 + 256)
        mt2[k] = mt1[:, lanes] + rm2[:, lanes]
    rm3[z] = mt2[colour]
    lax.fori_loop(1, 8, m3_start, 0)
    stage2(0)
    stage3(3)
    stage3(2)
    stage3(1)
    stage3(0)
    stage3(4)
    m3_all().wait_recv()
    grad = rm3[0]
    for p in range(1, 8):
        grad = grad + rm3[p]
    quarters[colour] = grad
    for k in range(3):
        m4_copy(k).start()
    m4_all().wait_recv()
    for k in range(4):
        lanes = slice(k * 256, k * 256 + 256)
        gmean_out[:, lanes] = quarters[k] - m_in[:, lanes].astype(F32)

    def p3_all(n, many):
        lanes = pl.ds(*parts[n])
        return remote(
            s2.at[pl.ds(0, many), :, lanes], r3.at[pl.ds(0, many), :, lanes], p3_s.at[n], p3_r.at[n], at(zp, xh, c)
        )

    def p3_wait(n):
        @pl.when(z >= firsts[n])
        def _():
            p3_all(n, 7).wait_recv()

    for n in range(5):
        p3_wait(n)
    data = r3[0].astype(F32)
    for p in range(1, 8):
        data = data + r3[p].astype(F32)
    column_ids = lax.broadcasted_iota(jnp.int32, (32, MB), 1)
    row_ids = lax.broadcasted_iota(jnp.int32, (32, MB), 0) + me * 32
    own_chol = lbuf[z, xh, c].astype(F32)
    on_diag = column_ids == row_ids
    diagonal = jnp.sum(jnp.where(on_diag, own_chol, 0.0), axis=1, keepdims=True)
    gchol_out[...] = (
        jnp.where(column_ids <= row_ids, data, 0.0) - own_chol + jnp.where(on_diag, 1.0 / diagonal, 0.0)
    )

    route_all().wait_send()
    gw.drain()
    gl.drain()

    slot = terms.at[pl.ds(0, 7)]
    remote(slot, slot, st_s, st_r.at[0], (me, (ib + 1) % 8)).wait_send()
    mean1.wait_send()
    mean2.wait_send()
    m3_all().wait_send()
    m4_all().wait_send()
    for n in range(4):
        p1_copy(n).wait_send()
    for n in range(5):
        p2_copy(n).wait_send()

        @pl.when(z >= firsts[n])
        def _():
            p3_all(n, 7 - firsts[n]).wait_send()

        @pl.when(z < firsts[n])
        def _():
            p3_all(n, 8 - firsts[n]).wait_send()


def body(
    obs_coords, obs_codes, route_plan, inducing_coords, inducing_bands, band_mix, lengthscales,
    class_scales, prior_factor, variational_chol, variational_mean,
):
    vmem = pl.BlockSpec(memory_space=pltpu.VMEM)
    whole = pl.BlockSpec(memory_space=pl.ANY)
    dma = pltpu.SemaphoreType.DMA
    return pl.pallas_call(
        kernel,
        out_shape=(
            pltpu.VMEM((C, ROWS), F32),
            pltpu.VMEM((32, MB), F32),
            pltpu.VMEM((C, MB), F32),
        ),
        in_specs=[whole] * 11,
        out_specs=(vmem, vmem, vmem),
        scratch_shapes=[
            pltpu.VMEM((2, 4096), F32),
            pltpu.VMEM((32, 128), jnp.int32),
            pltpu.VMEM((32, 32), jnp.int32),
            pltpu.VMEM((2, MB), F32),
            pltpu.VMEM((8, 128), jnp.int32),
            pltpu.VMEM((C, MB), BF16),
            pltpu.SMEM((NB, NB), F32), pltpu.SMEM((2,), F32), pltpu.SMEM((C,), F32),
            dma((11,)),
            pltpu.VMEM((2, 32, 128), F32),
            pltpu.VMEM((32, 4, 128), F32),
            pltpu.VMEM((32, 4, 128), F32),
            pltpu.VMEM((16, 8, 128), F32),
            pltpu.VMEM((8, 2, 256), F32),
            pltpu.VMEM((128, MB), BF16),
            pltpu.VMEM((2, MB), F32),
            pltpu.VMEM((16, MB), BF16),
            pltpu.VMEM((8, 2, 2, 32, MB), BF16),
            pltpu.VMEM((8, 2, 2, 32, MB), BF16),
            pltpu.VMEM((ROWS, MB), BF16),
            pltpu.VMEM((ROWS, MB), BF16),
            pltpu.VMEM((MB, ROWS), BF16),
            pltpu.VMEM((ROWS, MB), F32),
            pltpu.VMEM((ROWS, MB), BF16),
            pltpu.VMEM((ROWS, 128), F32),
            pltpu.VMEM((8, 8, 8, 256), F32),
            pltpu.VMEM((16, ROWS), BF16),
            pltpu.VMEM((8, 2, 2, 32, MB), BF16),
            pltpu.VMEM((8, 2, 32, MB), BF16),
            pltpu.VMEM((8, 2, 32, MB), BF16),
            pltpu.VMEM((8, 32, MB), BF16),
            pltpu.VMEM((8, 32, MB), BF16),
            pltpu.VMEM((8, 32, MB), BF16),
            pltpu.VMEM((8, MB), F32),
            pltpu.VMEM((8, MB), F32),
            pltpu.VMEM((4, 8, 256), F32),
            pltpu.VMEM((8, MB), F32),
            pltpu.VMEM((8, MB), F32),
            pltpu.VMEM((8, 8, 256), F32),
            pltpu.VMEM((4, 8, 256), F32),
            dma(()), dma(()), dma((8,)), dma((16,)), dma((8,)), dma((16,)),
            dma(()), dma((5,)),
            dma((4,)), dma((4,)), dma((5,)), dma((5,)), dma((5,)), dma((5,)),
            dma((2,)), dma((2,)), dma(()), dma(()), dma(()), dma(()),
        ],
        compiler_params=pltpu.CompilerParams(
            collective_id=0, has_side_effects=True, vmem_limit_bytes=60 << 20
        ),
        name="elbo_step",
    )(
        obs_coords, obs_codes.reshape(32, 128), route_plan, inducing_coords,
        inducing_bands.reshape(8, 128), band_mix, lengthscales, class_scales,
        prior_factor, variational_chol, variational_mean,
    )


def solution(mesh):
    placed = (
        P(None, "obs"), P("obs"), P(), P(None, "ind"), P("ind"), P(), P(), P(),
        P(("ind", "obs"), None), P(("ind", "obs"), None), P(None, "ind"),
    )
    return jax.shard_map(
        body,
        mesh=mesh,
        in_specs=placed,
        out_specs=(P(None, "obs"), P(("ind", "obs"), None), P(None, "ind")),
        check_vma=False,
    )
```
